32 devices in a mesh: vec: 4 (over y, core), dom: 8 (over z, x).
Axes of the slice: x: 2, y: 2, z: 4, core: 2. Of those that a mesh axis runs over, the one named last changes fastest.
Arguments:
- probe: float32 [16, 1024, 256], P('vec', 'dom'), may hold values from -5 to 5
- cheb_prev: float32 [16, 1024, 256], P('vec', 'dom'), may hold values from -6 to 6
- cheb_cur: float32 [16, 1024, 256], P('vec', 'dom'), may hold values from -6 to 6
- prior_moments: float32 [124, 1024, 256], P(None, ('dom', 'vec')), may hold values from -3 to 3
- site_terms: float32 [3, 1024, 128], P(None, 'dom'), may hold values from -0.3 to 0.3
- hop_kinds: float32 [8, 256, 256], replicated, may hold values from -0.09375 to 0.09375
- tile_kind_ids: int32 [1024, 4], P('dom'), may hold values from 0 to 7
- send_lists: int32 [8, 2, 48], P('dom'), may hold values from -1 to 127, as said below
- tile_cols: int32 [1024, 4], P('dom'), may hold values from 0 to 223, as said below
Outputs:
- next_prev: float32 [16, 1024, 256], P('vec', 'dom')
- next_cur: float32 [16, 1024, 256], P('vec', 'dom')
- new_moments: float32 [4, 1024, 256], P(None, ('dom', 'vec'))
- energy_map: float32 [512, 1024, 256], P(None, ('dom', 'vec'))
The draws below stay inside these ranges and needn't reach their ends.
Inputs may be any that keep to these rules, and one draw needn't show every extreme that they name: send_lists[d, 0] names local blocks of domain d sent to domain (d + 1) mod 8, send_lists[d, 1] those sent to domain (d - 1) mod 8; the valid entries come first and are distinct within the domain, the rest are -1; some domain sends 48 blocks one way. `tile_cols`: an entry e < 128 names the domain's own block e, 128 <= e < 176 names slot e - 128 of what the lower neighbour sends up, larger e slot e - 176 of what the upper neighbour sends down; only valid slots are named; link 0 of each block row is the block itself.
All inputs are finite; a program needn't handle non-finite values.
Results may differ from the reference program's by a relative error of at most 0.0001.
Values sent between devices are 32-bit elements; how exact they have to be, the bound alone decides.
No kernel may reach another device: no remote copies, remote signals or barrier semaphores. Data moves between devices by JAX's collectives and lax.ppermute only.
A program may use at most 128 MiB of HBM per device.

```python
import math
import jax
import jax.numpy as jnp
from jax import lax

BLOCK_SITES = 128
DOM_BLOCKS = 128
RIM = 48
LINKS = 4
KINDS = 8
VECS = 16
STEPS = 4
MOMENTS = 128
ENERGIES = 512
DOMAINS = 8
BLOCKS = 1024


def kpm_layout(key):
    base_key = jax.random.fold_in(key, 11)
    key_peak, key_counts, key_scores, key_category, key_raw = jax.random.split(base_key, 5)
    peak_domain = jax.random.randint(key_peak, (), 0, DOMAINS)
    counts = jax.random.randint(key_counts, (DOMAINS, 2), 1, RIM + 1)
    domain_ids = jnp.arange(DOMAINS, dtype=jnp.int32)
    counts = jnp.where((domain_ids == peak_domain)[:, None], RIM, counts)
    counts = counts.at[(peak_domain + 1) % DOMAINS, 0].set(1)
    block_ids = jnp.arange(DOM_BLOCKS, dtype=jnp.int32)
    scores = jax.random.randint(key_scores, (DOMAINS, DOM_BLOCKS), 0, 1 << 20) * DOM_BLOCKS + block_ids[None, :]
    scores = jnp.where((domain_ids[:, None] == peak_domain) & (block_ids[None, :] == DOM_BLOCKS - 1), -1, scores)
    ordering = jnp.argsort(scores, axis=1, stable=True).astype(jnp.int32)
    picked = jnp.stack([ordering[:, :RIM], ordering[:, RIM:2 * RIM]], axis=1)
    slot_ids = jnp.arange(RIM, dtype=jnp.int32)[None, None, :]
    send_rows = jnp.where(slot_ids < counts[:, :, None], picked, -1)
    lower_count = jnp.roll(counts[:, 0], 1)
    upper_count = jnp.roll(counts[:, 1], -1)
    category = jax.random.randint(key_category, (DOMAINS, DOM_BLOCKS, LINKS), 0, 3)
    raw_draw = jax.random.randint(key_raw, (DOMAINS, DOM_BLOCKS, LINKS), 0, 1 << 20)
    columns = jnp.where(category == 0, raw_draw % DOM_BLOCKS, jnp.where(category == 1, DOM_BLOCKS + raw_draw % lower_count[:, None, None], DOM_BLOCKS + RIM + raw_draw % upper_count[:, None, None]))
    columns = columns.at[:, :, 0].set(block_ids[None, :])
    forced_domain = (peak_domain - 1) % DOMAINS
    columns = columns.at[forced_domain, 0, LINKS - 1].set(DOM_BLOCKS + 2 * RIM - 1)
    return (send_rows.astype(jnp.int32), columns.reshape(DOMAINS * DOM_BLOCKS, LINKS).astype(jnp.int32))


def draw_send_lists(key, part):
    return kpm_layout(key)[0]


def draw_tile_cols(key, part):
    return kpm_layout(key)[1]


def place_ends(entries, stream_key, smallest, top_value):
    place = [jax.random.randint(jax.random.fold_in(stream_key, axis), (), 0, length) for axis, length in enumerate(entries.shape)]
    longest = entries.shape.index(max(entries.shape))
    beside = place[:longest] + [(place[longest] + 1) % entries.shape[longest]] + place[longest + 1:]
    return entries.at[tuple(place)].set(smallest).at[tuple(beside)].set(top_value)


def block_levels(stream_key, shape, cuts, least, top_value):
    gain = 1.0
    for dim, blocks in cuts:
        draws = jax.random.uniform(jax.random.fold_in(jax.random.fold_in(stream_key, 6), dim), (blocks,), jnp.float32, least / len(cuts), top_value / len(cuts))
        gain = gain * jnp.repeat(jnp.exp(draws), shape[dim] // blocks).reshape((-1,) + (1,) * (len(shape) - 1 - dim))
    return gain


def gaussian(key, shape, scale, reach, cuts=(), kind=jnp.bfloat16):
    values = scale * jax.random.normal(key, shape, jnp.float32)
    if cuts:
        values = values * block_levels(key, shape, cuts, -0.22, 0.18)
    return jnp.clip(values, -reach, reach).astype(kind)


def setup_inputs(seed: int = 0) -> dict:
    seeds = jax.random.split(jax.random.key(seed), 10)
    return {
        "probe": gaussian(seeds[0], (VECS, BLOCKS, 2 * BLOCK_SITES), 1.0, 5.0, ((0, 4), (1, 8)), jnp.float32),
        "cheb_prev": gaussian(seeds[1], (VECS, BLOCKS, 2 * BLOCK_SITES), 1.0, 6.0, ((0, 4), (1, 8)), jnp.float32),
        "cheb_cur": gaussian(seeds[2], (VECS, BLOCKS, 2 * BLOCK_SITES), 1.0, 6.0, ((0, 4), (1, 8)), jnp.float32),
        "prior_moments": gaussian(seeds[3], (MOMENTS - STEPS, BLOCKS, 2 * BLOCK_SITES), 0.3, 3.0, ((1, 32),), jnp.float32),
        "site_terms": jnp.clip(jax.random.uniform(seeds[4], (3, BLOCKS, BLOCK_SITES), jnp.float32, -0.3, 0.3) * block_levels(seeds[4], (3, BLOCKS, BLOCK_SITES), ((1, 8),), -0.4, 0.0), -0.3, 0.3),
        "hop_kinds": gaussian(seeds[5], (KINDS, 2 * BLOCK_SITES, 2 * BLOCK_SITES), (8 * LINKS * BLOCK_SITES) ** -0.5, 0.09375, (), jnp.float32),
        "tile_kind_ids": place_ends(jax.random.randint(seeds[6], (BLOCKS, LINKS), 0, KINDS), jax.random.fold_in(seeds[6], 1), 0, KINDS - 1).astype(jnp.int32),
        "send_lists": draw_send_lists(jax.random.fold_in(seeds[9], 71), 0),
        "tile_cols": draw_tile_cols(jax.random.fold_in(seeds[9], 71), 0),
    }


def jackson_table(moment_count, energy_count):
    indices = jnp.arange(moment_count, dtype=jnp.float32)
    denominator = moment_count + 1.0
    step_angle = math.pi / denominator
    damping = ((moment_count - indices + 1.0) * jnp.cos(step_angle * indices) + jnp.sin(step_angle * indices) * (math.cos(step_angle) / math.sin(step_angle))) / denominator
    weights = jnp.where(indices == 0, damping, 2.0 * damping)
    angles = math.pi * (jnp.arange(energy_count, dtype=jnp.float32) + 0.5) / energy_count
    return weights[None, :] * jnp.cos(angles[:, None] * indices[None, :])


def source_blocks(send_lists, tile_cols):
    domain_of = (jnp.arange(BLOCKS, dtype=jnp.int32) // DOM_BLOCKS)[:, None]
    lower_domain = (domain_of - 1) % DOMAINS
    upper_domain = (domain_of + 1) % DOMAINS
    lower_slot = jnp.clip(tile_cols - DOM_BLOCKS, 0, RIM - 1)
    upper_slot = jnp.clip(tile_cols - DOM_BLOCKS - RIM, 0, RIM - 1)
    lower_source = jnp.maximum(send_lists[lower_domain, 0, lower_slot], 0)
    upper_source = jnp.maximum(send_lists[upper_domain, 1, upper_slot], 0)
    result = jnp.where(tile_cols < DOM_BLOCKS, domain_of * DOM_BLOCKS + tile_cols,
                       jnp.where(tile_cols < DOM_BLOCKS + RIM, lower_domain * DOM_BLOCKS + lower_source,
                                 upper_domain * DOM_BLOCKS + upper_source))
    return result.astype(jnp.int32)


def reference(probe, cheb_prev, cheb_cur, prior_moments, site_terms, hop_kinds, tile_kind_ids, send_lists, tile_cols):
    row_width = 2 * BLOCK_SITES
    sources = source_blocks(send_lists, tile_cols)
    onehot = (tile_kind_ids[:, :, None] == jnp.arange(KINDS, dtype=jnp.int32)[None, None, :]).astype(jnp.float32)
    kinds_flat = hop_kinds.reshape(KINDS * row_width, row_width)
    level_energy = site_terms[0]
    field_z = site_terms[1]
    field_x = site_terms[2]

    def per_vector(gathered_one):
        mixture = jnp.einsum("bkn,bki->bni", onehot, gathered_one, precision=lax.Precision.HIGHEST)
        mixture = mixture.reshape(BLOCKS, KINDS * row_width)
        return jnp.dot(mixture, kinds_flat, precision=lax.Precision.HIGHEST)

    def hamilton(current):
        hopping = lax.map(per_vector, current[:, sources])
        spin_up = current[:, :, :BLOCK_SITES]
        spin_down = current[:, :, BLOCK_SITES:]
        onsite = jnp.concatenate([(level_energy + field_z) * spin_up + field_x * spin_down,
                                  (level_energy - field_z) * spin_down + field_x * spin_up], axis=2)
        return hopping + onsite

    previous, current = cheb_prev, cheb_cur
    collected = []
    for iteration in range(STEPS):
        following = 2.0 * hamilton(current) - previous
        previous, current = current, following
        collected.append(jnp.sum(probe * following, axis=0) / VECS)
    new_moments = jnp.stack(collected, axis=0)
    moments = jnp.concatenate([prior_moments, new_moments], axis=0)
    cosine_table = jackson_table(MOMENTS, ENERGIES)
    energy_map = jnp.dot(cosine_table, moments.reshape(MOMENTS, BLOCKS * row_width), precision=lax.Precision.HIGHEST)
    return previous, current, new_moments, energy_map.reshape(ENERGIES, BLOCKS, row_width)
```

```python
import functools
import math

import jax
import jax.numpy as jnp
import numpy as np
from jax import lax
from jax.experimental import pallas as pl
from jax.experimental.pallas import tpu as pltpu
from jax.sharding import PartitionSpec as P

ENERGIES = 512
STEPS = 4
F32 = jnp.float32
BF16 = jnp.bfloat16
VMEM_LIMIT = 24 * 1024 * 1024


def split(x):
    high = x.astype(BF16)
    return high, (x - high.astype(F32)).astype(BF16)


def dot(a, b):
    return jnp.dot(a, b, preferred_element_type=F32)


def jackson_split(moment_count, energy_count):
    m = np.arange(moment_count, dtype=np.float64)
    step = math.pi / (moment_count + 1.0)
    damping = (
        (moment_count - m + 1.0) * np.cos(step * m) + np.sin(step * m) / math.tan(step)
    ) / (moment_count + 1.0)
    weights = np.where(m == 0, damping, 2.0 * damping)
    angles = math.pi * (np.arange(energy_count) + 0.5) / energy_count
    table = (weights[None, :] * np.cos(angles[:, None] * m[None, :])).astype(np.float32)
    high = table.astype(BF16)
    low = (table - high.astype(np.float32)).astype(BF16)
    return np.concatenate([high, low], axis=1), high


def vmem():
    return pl.BlockSpec(memory_space=pltpu.VMEM)


def smem():
    return pl.BlockSpec(memory_space=pltpu.SMEM)


def params(limit=VMEM_LIMIT):
    return pltpu.CompilerParams(vmem_limit_bytes=limit)


def cost(flops, size):
    return pl.CostEstimate(flops=int(flops), bytes_accessed=int(size), transcendentals=0)


def gather_rows(onehot, value):
    high, low = split(value)
    return dot(onehot, jnp.concatenate([high, low], axis=0))


def first_kernel(rim, vecs, parity_ref, lists_ref, cur_ref, pick_ref, *sends):
    blocks = cur_ref.shape[1]
    width = cur_ref.shape[2]
    lists = lists_ref[0]
    even = parity_ref[0] == 0
    rows = lax.broadcasted_iota(jnp.int32, (rim, rim), 0)
    lanes = lax.broadcasted_iota(jnp.int32, (rim, rim), 1)
    slots = lax.broadcasted_iota(jnp.int32, (rim, blocks), 1)
    for half in range(2):
        mine = lists[half : half + 1]
        other = lists[1 - half : 2 - half]
        chosen = jnp.where(even, mine, other)
        spread = jnp.where(rows == lanes, chosen, 0).astype(F32)
        column = jnp.sum(spread, axis=1, keepdims=True).astype(jnp.int32)
        onehot = jnp.where(slots == column, 1.0, 0.0).astype(BF16)
        pick_ref[pl.ds(half * rim, rim), 0:blocks] = onehot
        pick_ref[pl.ds(half * rim, rim), blocks : 2 * blocks] = onehot
    pick = pick_ref[...]
    for v in range(cur_ref.shape[0]):
        chunk, place = divmod(v, vecs)
        got = gather_rows(pick, cur_ref[v])
        for half in range(2):
            sends[2 * chunk + half][:, place * width : (place + 1) * width] = got[
                half * rim : (half + 1) * rim
            ]


def prep_kernel(rim, parity_ref, cols_ref, ids_ref, kinds_ref, mix_ref, high_ref, low_ref):
    blocks, links = cols_ref.shape
    kind_count, width = kinds_ref.shape[:2]
    padded = mix_ref.shape[1] // 2
    even = parity_ref[0] == 0
    lanes = lax.broadcasted_iota(jnp.int32, (blocks, padded), 1)
    hits = []
    for k in range(links):
        e = cols_ref[:, k : k + 1]
        crossed = jnp.where(e < blocks + rim, e + rim, e - rim)
        e = jnp.where(jnp.logical_and(even, e >= blocks), crossed, e)
        hits.append(jnp.where(lanes == e, 1.0, 0.0))
    for n in range(kind_count):
        total = jnp.zeros((blocks, padded), F32)
        for k in range(links):
            total += jnp.where(ids_ref[:, k : k + 1] == n, hits[k], 0.0)
        total = total.astype(BF16)
        mix_ref[n * blocks : (n + 1) * blocks, 0:padded] = total
        mix_ref[n * blocks : (n + 1) * blocks, padded : 2 * padded] = total
        high, low = split(2.0 * kinds_ref[n])
        high_ref[n * width : (n + 1) * width] = high
        low_ref[n * width : (n + 1) * width] = low


def step_kernel(
    cfg,
    index_ref,
    mix_ref,
    high_ref,
    low_ref,
    pick_ref,
    site_ref,
    cur_ref,
    prev_ref,
    probe_ref,
    recv_a,
    recv_b,
    *rest,
):
    chunk, last, add_partial, older, has_alias = cfg
    rest = list(rest)
    partial_in = rest.pop(0) if add_partial else None
    olders = [rest.pop(0) for _ in range(older)]
    if has_alias:
        rest.pop(0)
    out_ref = rest.pop(0)
    if last:
        partial_out = rest.pop(0)
        keep_ref = rest.pop(0) if older else None
        give_ref = rest.pop(0) if older else None
    else:
        send_a, send_b, partial_out = rest.pop(0), rest.pop(0), rest.pop(0)
    source, mixed = rest
    vecs, blocks, width = cur_ref.shape
    rim = recv_a.shape[0]
    padded = source.shape[1] // 2
    kind_count = mix_ref.shape[0] // blocks
    spin = width // 2
    for v in range(vecs):
        columns = slice(v * width, (v + 1) * width)
        pieces = [cur_ref[v], recv_a[:, columns], recv_b[:, columns]]
        used = blocks + 2 * rim
        if used < padded:
            pieces.append(jnp.zeros((padded - used, width), F32))
        high, low = split(jnp.concatenate(pieces, axis=0))
        source[v, 0:padded] = high
        source[v, padded : 2 * padded] = low
    for v in range(vecs):
        mixture = dot(mix_ref[...], source[v])
        high, low = split(mixture)
        for n in range(kind_count):
            columns = slice(n * width, (n + 1) * width)
            rows = slice(n * blocks, (n + 1) * blocks)
            mixed[v * blocks : (v + 1) * blocks, columns] = high[rows]
            mixed[(vecs + v) * blocks : (vecs + v + 1) * blocks, columns] = low[rows]
    count = vecs * blocks
    both = dot(mixed[...], high_ref[...])
    hopping = both[:count] + both[count:] + dot(mixed[:count], low_ref[...])
    diag_up = 2.0 * (site_ref[0] + site_ref[1])
    diag_down = 2.0 * (site_ref[0] - site_ref[1])
    cross = 2.0 * site_ref[2]
    partial = partial_in[...] if add_partial else None
    for v in range(vecs):
        here = cur_ref[v]
        up = here[:, :spin]
        down = here[:, spin:]
        onsite = jnp.concatenate(
            [diag_up * up + cross * down, diag_down * down + cross * up], axis=1
        )
        following = hopping[v * blocks : (v + 1) * blocks] + onsite - prev_ref[v]
        out_ref[v] = following
        term = probe_ref[v] * following
        partial = term if partial is None else partial + term
        if not last:
            got = gather_rows(pick_ref[...], following)
            send_a[:, v * width : (v + 1) * width] = got[:rim]
            send_b[:, v * width : (v + 1) * width] = got[rim:]
    partial_out[...] = partial
    if last and older:
        groups, cores = index_ref[2], 2
        quarter = keep_ref.shape[2]
        core = index_ref[1]
        for s in range(older + 1):
            ref = olders[s] if s < older else partial_out
            for y in range(keep_ref.shape[1]):
                base = y * cores * quarter
                keep_ref[s, y] = ref[pl.ds(pl.multiple_of(base + core * quarter, quarter), quarter)]
                give_ref[s, y] = ref[
                    pl.ds(pl.multiple_of(base + (1 - core) * quarter, quarter), quarter)
                ]


def fold_kernel(index_ref, keep_ref, got_ref, mine_ref, give_ref):
    y = index_ref[2]
    mine_ref[...] = keep_ref[:, y] + got_ref[:, y]
    give_ref[...] = keep_ref[:, 1 - y] + got_ref[:, 1 - y]


def energy_kernel(vector_total, both_ref, high_ref, prior_ref, mine_ref, got_ref, new_ref, map_ref, moments):
    prior_count, group, lanes = prior_ref.shape
    steps = mine_ref.shape[0]
    energies = both_ref.shape[0]
    new = (mine_ref[...] + got_ref[...]) * (1.0 / vector_total)
    new_ref[...] = new
    moments[0 : prior_count * group] = prior_ref[...].reshape(prior_count * group, lanes)
    moments[prior_count * group :] = new.reshape(steps * group, lanes)
    flat = map_ref.reshape(energies * group, lanes)
    for b in range(0, group, 2):
        pair = [moments[pl.ds(b + i, prior_count + steps, stride=group)] for i in range(2)]
        high, low = split(jnp.concatenate(pair, axis=1))
        value = dot(both_ref[...], jnp.concatenate([high, high], axis=0)) + dot(high_ref[...], low)
        for i in range(2):
            flat[pl.ds(b + i, energies, stride=group)] = value[:, i * lanes : (i + 1) * lanes]


def per_device(
    probe,
    cheb_prev,
    cheb_cur,
    prior_moments,
    site_terms,
    hop_kinds,
    tile_kind_ids,
    send_lists,
    tile_cols,
):
    vec_dev, blocks, width = cheb_cur.shape
    kind_count = hop_kinds.shape[0]
    groups = lax.axis_size("vec")
    domains = lax.axis_size("dom")
    rim = send_lists.shape[2]
    chunks = 2
    vecs = vec_dev // chunks
    quarter = blocks // groups
    padded = -(-(blocks + 2 * rim) // 256) * 256
    swap_a = [(i, i ^ 1) for i in range(domains)]
    swap_b = [(i, (i + 1) % domains if i % 2 else (i - 1) % domains) for i in range(domains)]
    vec_index = lax.axis_index("vec")
    index = jnp.stack([lax.axis_index("dom") % 2, vec_index % 2, vec_index // 2]).astype(jnp.int32)

    rows = jax.ShapeDtypeStruct((rim, vecs * width), F32)
    first = pl.pallas_call(
        functools.partial(first_kernel, rim, vecs),
        out_shape=[jax.ShapeDtypeStruct((2 * rim, 2 * blocks), BF16)] + [rows] * (2 * chunks),
        in_specs=[smem(), vmem(), vmem()],
        out_specs=[vmem()] * (1 + 2 * chunks),
        compiler_params=params(),
        cost_estimate=cost(1e8, 1e6),
        name="first_sends",
    )(index, send_lists, cheb_cur)
    pick, sends = first[0], list(first[1:])

    def exchange(a, b):
        got_b = lax.ppermute(b, "dom", swap_b)
        got_a = lax.ppermute(a, "dom", swap_a)
        return got_a, got_b

    received = [exchange(sends[2 * c], sends[2 * c + 1]) for c in range(chunks)]

    mix, high, low = pl.pallas_call(
        functools.partial(prep_kernel, rim),
        out_shape=[
            jax.ShapeDtypeStruct((kind_count * blocks, 2 * padded), BF16),
            jax.ShapeDtypeStruct((kind_count * width, width), BF16),
            jax.ShapeDtypeStruct((kind_count * width, width), BF16),
        ],
        in_specs=[smem()] + [vmem()] * 3,
        out_specs=[vmem()] * 3,
        compiler_params=params(),
        cost_estimate=cost(1e7, 8e6),
        name="tables",
    )(index, tile_cols, tile_kind_ids, hop_kinds)

    def chunk_spec(c):
        return pl.BlockSpec((vecs, blocks, width), lambda i: (c, 0, 0))

    whole = chunk_spec(0)
    partial_shape = jax.ShapeDtypeStruct((blocks, width), F32)
    rows_spec = pl.BlockSpec((rim, vecs * width), lambda i: (0, 0))
    partial_spec = pl.BlockSpec((blocks, width), lambda i: (0, 0))
    full_shape = jax.ShapeDtypeStruct((vec_dev, blocks, width), F32)
    chunk_shape = jax.ShapeDtypeStruct((vecs, blocks, width), F32)

    current = [(cheb_cur, c) for c in range(chunks)]
    previous = [(cheb_prev, c) for c in range(chunks)]
    partials = []
    keep = give = None
    for s in range(STEPS):
        last = s == STEPS - 1
        emit = s >= STEPS - 2
        partial = None
        buffer = None
        for c in range(chunks):
            final = last and c == chunks - 1
            args = [index, mix, high, low, pick, site_terms, current[c][0], previous[c][0], probe]
            specs = [
                smem(),
                pl.BlockSpec((kind_count * blocks, 2 * padded), lambda i: (0, 0)),
                pl.BlockSpec((kind_count * width, width), lambda i: (0, 0)),
                pl.BlockSpec((kind_count * width, width), lambda i: (0, 0)),
                pl.BlockSpec((2 * rim, 2 * blocks), lambda i: (0, 0)),
                pl.BlockSpec(site_terms.shape, lambda i: (0, 0, 0)),
                chunk_spec(current[c][1]),
                chunk_spec(previous[c][1]),
                chunk_spec(c),
                rows_spec,
                rows_spec,
            ]
            args += list(received[c])
            if partial is not None:
                args.append(partial)
                specs.append(partial_spec)
            older = len(partials) if final else 0
            if older:
                args += partials
                specs += [partial_spec] * older
            aliases = {}
            if emit and buffer is not None:
                aliases = {len(args): 0}
                args.append(buffer)
                specs.append(pl.BlockSpec(memory_space=pl.ANY))
            outs = [full_shape if emit else chunk_shape]
            out_specs = [chunk_spec(c) if emit else whole]
            if not last:
                outs += [rows, rows]
                out_specs += [rows_spec, rows_spec]
            outs.append(partial_shape)
            out_specs.append(partial_spec)
            if older:
                pair = jax.ShapeDtypeStruct((older + 1, groups // 2, quarter, width), F32)
                outs += [pair, pair]
                out_specs += [pl.BlockSpec(pair.shape, lambda i: (0, 0, 0, 0))] * 2
            result = pl.pallas_call(
                functools.partial(
                    step_kernel, (c, last, partial is not None, older, bool(aliases))
                ),
                out_shape=outs,
                grid=(1,),
                in_specs=specs,
                out_specs=out_specs,
                scratch_shapes=[
                    pltpu.VMEM((vecs, 2 * padded, width), BF16),
                    pltpu.VMEM((2 * vecs * blocks, kind_count * width), BF16),
                ],
                input_output_aliases=aliases,
                compiler_params=params(),
                cost_estimate=cost(1.5e9, 5e6),
                name=f"step{s}_{c}",
            )(*args)
            following = result[0]
            if emit:
                buffer = following
            partial = result[1] if last else result[3]
            previous[c] = current[c]
            current[c] = (following, c if emit else 0)
            if not last:
                received[c] = exchange(result[1], result[2])
            elif older:
                keep, give = result[2], result[3]
        if emit:
            for c in range(chunks):
                current[c] = (buffer, c)
        partials.append(partial)

    got = lax.ppermute(give, "vec", [(i, i ^ 1) for i in range(groups)])
    piece = jax.ShapeDtypeStruct((STEPS, quarter, width), F32)
    mine, give = pl.pallas_call(
        fold_kernel,
        out_shape=[piece, piece],
        in_specs=[smem(), vmem(), vmem()],
        out_specs=[vmem(), vmem()],
        compiler_params=params(),
        cost_estimate=cost(1e5, 1e6),
        name="fold",
    )(index, keep, got)
    got = lax.ppermute(give, "vec", [(i, i ^ 2) for i in range(groups)])

    prior_count = prior_moments.shape[0]
    moment_count = prior_count + STEPS
    both, top = jackson_split(moment_count, ENERGIES)
    group, lanes = 8, 128
    small = pl.BlockSpec((STEPS, group, lanes), lambda i, h: (0, i, h))
    new_moments, energy_map = pl.pallas_call(
        functools.partial(energy_kernel, vec_dev * groups),
        out_shape=[piece, jax.ShapeDtypeStruct((ENERGIES, quarter, width), F32)],
        grid=(quarter // group, width // lanes),
        in_specs=[
            pl.BlockSpec((ENERGIES, 2 * moment_count), lambda i, h: (0, 0)),
            pl.BlockSpec((ENERGIES, moment_count), lambda i, h: (0, 0)),
            pl.BlockSpec((prior_count, group, lanes), lambda i, h: (0, i, h)),
            small,
            small,
        ],
        out_specs=[small, pl.BlockSpec((ENERGIES, group, lanes), lambda i, h: (0, i, h))],
        scratch_shapes=[pltpu.VMEM((moment_count * group, lanes), F32)],
        compiler_params=params(),
        cost_estimate=cost(4e9, 2.2e7),
        name="energy",
    )(jnp.asarray(both), jnp.asarray(top), prior_moments, mine, got)
    return current_outputs(previous, current) + (new_moments, energy_map)


def current_outputs(previous, current):
    return previous[0][0], current[0][0]


def solution(mesh):
    return jax.shard_map(
        per_device,
        mesh=mesh,
        in_specs=(
            P("vec", "dom", None),
            P("vec", "dom", None),
            P("vec", "dom", None),
            P(None, ("dom", "vec"), None),
            P(None, "dom", None),
            P(),
            P("dom", None),
            P("dom", None, None),
            P("dom", None),
        ),
        out_specs=(
            P("vec", "dom", None),
            P("vec", "dom", None),
            P(None, ("dom", "vec"), None),
            P(None, ("dom", "vec"), None),
        ),
        check_vma=False,
    )
```

```python
import functools
import math

import jax
import jax.numpy as jnp
import numpy as np
from jax import lax
from jax.experimental import pallas as pl
from jax.experimental.pallas import tpu as pltpu
from jax.sharding import PartitionSpec as P

ENERGIES = 512
STEPS = 4
F32 = jnp.float32
BF16 = jnp.bfloat16
VMEM_LIMIT = 24 * 1024 * 1024


def split(x):
    high = x.astype(BF16)
    return high, (x - high.astype(F32)).astype(BF16)


def dot(a, b):
    return jnp.dot(a, b, preferred_element_type=F32)


def jackson_split(moment_count, energy_count):
    m = np.arange(moment_count, dtype=np.float64)
    step = math.pi / (moment_count + 1.0)
    damping = (
        (moment_count - m + 1.0) * np.cos(step * m) + np.sin(step * m) / math.tan(step)
    ) / (moment_count + 1.0)
    weights = np.where(m == 0, damping, 2.0 * damping)
    angles = math.pi * (np.arange(energy_count // 2) + 0.5) / energy_count
    table = (weights[None, :] * np.cos(angles[:, None] * m[None, :])).astype(np.float32)
    halves = []
    for parity in range(2):
        part = table[:, parity::2]
        high = part.astype(BF16)
        low = (part - high.astype(np.float32)).astype(BF16)
        halves.append(np.concatenate([high, low, high, low], axis=1))
    return halves


def vmem():
    return pl.BlockSpec(memory_space=pltpu.VMEM)


def smem():
    return pl.BlockSpec(memory_space=pltpu.SMEM)


def params(limit=VMEM_LIMIT):
    return pltpu.CompilerParams(vmem_limit_bytes=limit)


def cost(flops, size):
    return pl.CostEstimate(flops=int(flops), bytes_accessed=int(size), transcendentals=0)


def gather_rows(onehot, value):
    high, low = split(value)
    return dot(onehot, jnp.concatenate([high, low], axis=0))


def any_space():
    return pl.BlockSpec(memory_space=pl.ANY)


def first_kernel(rim, vecs, index_ref, lists_hbm, cur_hbm, pick_ref, cur_ref, *rest):
    sends, (lists_ref, sems) = rest[:-2], rest[-2:]
    count, blocks, width = cur_ref.shape
    list_copy = pltpu.make_async_copy(lists_hbm, lists_ref, sems.at[count])
    list_copy.start()
    copies = [pltpu.make_async_copy(cur_hbm.at[v], cur_ref.at[v], sems.at[v]) for v in range(count)]
    for copy in copies:
        copy.start()
    list_copy.wait()
    lists = lists_ref[0]
    even = index_ref[0] == 0
    rows = lax.broadcasted_iota(jnp.int32, (rim, rim), 0)
    lanes = lax.broadcasted_iota(jnp.int32, (rim, rim), 1)
    slots = lax.broadcasted_iota(jnp.int32, (rim, blocks), 1)
    for half in range(2):
        mine = lists[half : half + 1]
        other = lists[1 - half : 2 - half]
        chosen = jnp.where(even, mine, other)
        spread = jnp.where(rows == lanes, chosen, 0).astype(F32)
        column = jnp.sum(spread, axis=1, keepdims=True).astype(jnp.int32)
        onehot = jnp.where(slots == column, 1.0, 0.0).astype(BF16)
        pick_ref[pl.ds(half * rim, rim), 0:blocks] = onehot
        pick_ref[pl.ds(half * rim, rim), blocks : 2 * blocks] = onehot
    pick = pick_ref[...]
    for v in range(count):
        chunk, place = divmod(v, vecs)
        copies[v].wait()
        got = gather_rows(pick, cur_ref[v])
        for half in range(2):
            sends[2 * chunk + half][:, place * width : (place + 1) * width] = got[
                half * rim : (half + 1) * rim
            ]


def prep_kernel(
    rim,
    index_ref,
    cols_ref,
    ids_ref,
    kinds_hbm,
    prev_hbm,
    probe_hbm,
    site_hbm,
    mix_ref,
    high_ref,
    low_ref,
    prev_ref,
    probe_ref,
    site_ref,
    kinds,
    sems,
):
    links, blocks = cols_ref.shape
    kind_count, width = kinds.shape[:2]
    padded = mix_ref.shape[1] // 2
    copies = [
        pltpu.make_async_copy(kinds_hbm.at[n], kinds.at[n], sems.at[n]) for n in range(kind_count)
    ]
    fetched = ((prev_hbm, prev_ref), (probe_hbm, probe_ref), (site_hbm, site_ref))
    for i, (source, target) in enumerate(fetched):
        copies.append(pltpu.make_async_copy(source, target, sems.at[kind_count + i]))
    for copy in copies:
        copy.start()
    even = index_ref[0] == 0
    rows = lax.broadcasted_iota(jnp.int32, (padded, blocks), 0)
    corner = lax.broadcasted_iota(jnp.int32, (blocks, blocks), 0)
    diagonal = corner == lax.broadcasted_iota(jnp.int32, (blocks, blocks), 1)
    identity = jnp.where(diagonal, 1.0, 0.0).astype(BF16)
    e = cols_ref[...]
    crossed = jnp.where(e < blocks + rim, e + rim, e - rim)
    e = jnp.where(jnp.logical_and(even, e >= blocks), crossed, e)
    ids = ids_ref[...]
    for n in range(kind_count):
        mine = jnp.where(ids == n, e, -1)
        total = jnp.zeros((padded, blocks), F32)
        for k in range(links):
            total += jnp.where(rows == mine[k : k + 1], 1.0, 0.0)
        turned = lax.dot_general(
            identity, total.astype(BF16), (((1,), (1,)), ((), ())), preferred_element_type=F32
        ).astype(BF16)
        mix_ref[n * blocks : (n + 1) * blocks, 0:padded] = turned
        mix_ref[n * blocks : (n + 1) * blocks, padded : 2 * padded] = turned
    for n in range(kind_count):
        copies[n].wait()
        high, low = split(2.0 * kinds[n])
        high_ref[n * width : (n + 1) * width] = high
        low_ref[n * width : (n + 1) * width] = low
    for copy in copies[kind_count:]:
        copy.wait()


def step_kernel(
    cfg,
    index_ref,
    mix_ref,
    high_ref,
    low_ref,
    pick_ref,
    site_ref,
    cur_ref,
    prev_ref,
    probe_ref,
    recv_a,
    recv_b,
    *rest,
):
    vecs, cur_at, prev_at, own_at, last, add_partial, older, aliased = cfg
    rest = list(rest)
    partial_in = rest.pop(0) if add_partial else None
    olders = [rest.pop(0) for _ in range(older)]
    rest = rest[aliased:]
    if last:
        prev_out, out_hbm, partial_out = rest.pop(0), rest.pop(0), rest.pop(0)
        keep_ref = rest.pop(0) if older else None
        give_ref = rest.pop(0) if older else None
        source, mixed, out_ref, sems = rest
    else:
        out_ref, send_a, send_b, partial_out = rest[:4]
        source, mixed = rest[4:]
    blocks, width = cur_ref.shape[1:]
    rim = recv_a.shape[0]
    padded = source.shape[1] // 2
    kind_count = mix_ref.shape[0] // blocks
    spin = width // 2
    copies = []
    if last:
        copies.append(
            pltpu.make_async_copy(
                cur_ref.at[pl.ds(cur_at, vecs)], prev_out.at[pl.ds(own_at, vecs)], sems.at[vecs]
            )
        )
        copies[0].start()
    for v in range(vecs):
        columns = slice(v * width, (v + 1) * width)
        pieces = [cur_ref[cur_at + v], recv_a[:, columns], recv_b[:, columns]]
        used = blocks + 2 * rim
        if used < padded:
            pieces.append(jnp.zeros((padded - used, width), F32))
        high, low = split(jnp.concatenate(pieces, axis=0))
        source[v, 0:padded] = high
        source[v, padded : 2 * padded] = low
    for v in range(vecs):
        mixture = dot(mix_ref[...], source[v])
        high, low = split(mixture)
        for n in range(kind_count):
            columns = slice(n * width, (n + 1) * width)
            rows = slice(n * blocks, (n + 1) * blocks)
            mixed[v * blocks : (v + 1) * blocks, columns] = high[rows]
            mixed[(vecs + v) * blocks : (vecs + v + 1) * blocks, columns] = low[rows]
    count = vecs * blocks
    both = dot(mixed[...], high_ref[...])
    hopping = both[:count] + both[count:] + dot(mixed[:count], low_ref[...])
    diag_up = 2.0 * (site_ref[0] + site_ref[1])
    diag_down = 2.0 * (site_ref[0] - site_ref[1])
    cross = 2.0 * site_ref[2]
    partial = partial_in[...] if add_partial else None
    for v in range(vecs):
        here = cur_ref[cur_at + v]
        up = here[:, :spin]
        down = here[:, spin:]
        onsite = jnp.concatenate(
            [diag_up * up + cross * down, diag_down * down + cross * up], axis=1
        )
        following = hopping[v * blocks : (v + 1) * blocks] + onsite - prev_ref[prev_at + v]
        out_ref[v] = following
        if last:
            copies.append(pltpu.make_async_copy(out_ref.at[v], out_hbm.at[own_at + v], sems.at[v]))
            copies[-1].start()
        term = probe_ref[own_at + v] * following
        partial = term if partial is None else partial + term
        if not last:
            got = gather_rows(pick_ref[...], following)
            send_a[:, v * width : (v + 1) * width] = got[:rim]
            send_b[:, v * width : (v + 1) * width] = got[rim:]
    partial_out[...] = partial
    if last and older:
        cores = 2
        quarter = keep_ref.shape[2]
        core = index_ref[1]
        for s in range(older + 1):
            ref = olders[s] if s < older else partial_out
            for y in range(keep_ref.shape[1]):
                base = y * cores * quarter
                keep_ref[s, y] = ref[pl.ds(pl.multiple_of(base + core * quarter, quarter), quarter)]
                give_ref[s, y] = ref[
                    pl.ds(pl.multiple_of(base + (1 - core) * quarter, quarter), quarter)
                ]
    for copy in copies:
        copy.wait()


def fold_kernel(index_ref, keep_ref, got_ref, mine_ref, give_ref):
    y = index_ref[2]
    mine_ref[...] = keep_ref[:, y] + got_ref[:, y]
    give_ref[...] = keep_ref[:, 1 - y] + got_ref[:, 1 - y]


def energy_kernel(vector_total, even_ref, odd_ref, prior_ref, mine_ref, got_ref, new_ref, map_ref, moments):
    prior_count, group, lanes = prior_ref.shape
    steps = mine_ref.shape[0]
    half = even_ref.shape[0]
    pairs = (prior_count + steps) // 2
    new = (mine_ref[...] + got_ref[...]) * (1.0 / vector_total)
    new_ref[...] = new
    moments[0 : prior_count * group] = prior_ref[...].reshape(prior_count * group, lanes)
    moments[prior_count * group :] = new.reshape(steps * group, lanes)
    flat = map_ref.reshape(2 * half * group, lanes)
    flip = 7 - lax.broadcasted_iota(jnp.int32, (8, lanes), 0)
    for b in range(0, group, 2):
        sums = []
        for parity, table in ((0, even_ref), (1, odd_ref)):
            pair = [
                moments[pl.ds(parity * group + b + i, pairs, stride=2 * group)] for i in range(2)
            ]
            high, low = split(jnp.concatenate(pair, axis=1))
            sums.append(dot(table[...], jnp.concatenate([high, high, low, low], axis=0)))
        plus = sums[0] + sums[1]
        minus = sums[0] - sums[1]
        for i in range(2):
            columns = slice(i * lanes, (i + 1) * lanes)
            flat[pl.ds(b + i, half, stride=group)] = plus[:, columns]
            for r in range(0, half, 8):
                turned = jnp.take_along_axis(minus[r : r + 8, columns], flip, axis=0)
                top = 2 * half - 8 - r
                flat[pl.ds(top * group + b + i, 8, stride=group)] = turned


def per_device(
    probe,
    cheb_prev,
    cheb_cur,
    prior_moments,
    site_terms,
    hop_kinds,
    tile_kind_ids,
    send_lists,
    tile_cols,
):
    vec_dev, blocks, width = cheb_cur.shape
    kind_count = hop_kinds.shape[0]
    groups = lax.axis_size("vec")
    domains = lax.axis_size("dom")
    rim = send_lists.shape[2]
    chunks = 2
    vecs = vec_dev // chunks
    quarter = blocks // groups
    padded = -(-(blocks + 2 * rim) // 256) * 256
    swap_a = [(i, i ^ 1) for i in range(domains)]
    swap_b = [(i, (i + 1) % domains if i % 2 else (i - 1) % domains) for i in range(domains)]
    vec_index = lax.axis_index("vec")
    index = jnp.stack([lax.axis_index("dom") % 2, vec_index % 2, vec_index // 2]).astype(jnp.int32)

    rows = jax.ShapeDtypeStruct((rim, vecs * width), F32)
    full_shape = jax.ShapeDtypeStruct((vec_dev, blocks, width), F32)
    chunk_shape = jax.ShapeDtypeStruct((vecs, blocks, width), F32)
    first = pl.pallas_call(
        functools.partial(first_kernel, rim, vecs),
        out_shape=[jax.ShapeDtypeStruct((2 * rim, 2 * blocks), BF16), full_shape]
        + [rows] * (2 * chunks),
        in_specs=[smem(), any_space(), any_space()],
        out_specs=[vmem()] * (2 + 2 * chunks),
        scratch_shapes=[
            pltpu.VMEM(send_lists.shape, jnp.int32),
            pltpu.SemaphoreType.DMA((vec_dev + 1,)),
        ],
        compiler_params=params(),
        cost_estimate=cost(1e8, 1e6),
        name="first_sends",
    )(index, send_lists, cheb_cur)
    pick, cur_held, sends = first[0], first[1], list(first[2:])

    def exchange(a, b):
        got_b = lax.ppermute(b, "dom", swap_b)
        got_a = lax.ppermute(a, "dom", swap_a)
        return got_a, got_b

    received = [exchange(sends[2 * c], sends[2 * c + 1]) for c in range(chunks)]

    mix, high, low, prev_held, probe_held, site_held = pl.pallas_call(
        functools.partial(prep_kernel, rim),
        out_shape=[
            jax.ShapeDtypeStruct((kind_count * blocks, 2 * padded), BF16),
            jax.ShapeDtypeStruct((kind_count * width, width), BF16),
            jax.ShapeDtypeStruct((kind_count * width, width), BF16),
            full_shape,
            full_shape,
            jax.ShapeDtypeStruct(site_terms.shape, F32),
        ],
        in_specs=[smem(), vmem(), vmem()] + [any_space()] * 4,
        out_specs=[vmem()] * 6,
        scratch_shapes=[
            pltpu.VMEM(hop_kinds.shape, F32),
            pltpu.SemaphoreType.DMA((kind_count + 3,)),
        ],
        compiler_params=params(),
        cost_estimate=cost(1e7, 8e6),
        name="tables",
    )(index, tile_cols.T, tile_kind_ids.T, hop_kinds, cheb_prev, probe, site_terms)

    partial_shape = jax.ShapeDtypeStruct((blocks, width), F32)
    current = [(cur_held, c * vecs) for c in range(chunks)]
    previous = [(prev_held, c * vecs) for c in range(chunks)]
    partials = []
    buffers = []
    for s in range(STEPS):
        last = s == STEPS - 1
        partial = None
        for c in range(chunks):
            args = [index, mix, high, low, pick, site_held]
            args += [current[c][0], previous[c][0], probe_held, *received[c]]
            specs = [smem()] + [vmem()] * (len(args) - 1)
            older = len(partials) if last and c == chunks - 1 else 0
            extra = ([] if partial is None else [partial]) + (partials if older else [])
            args += extra
            specs += [vmem()] * len(extra)
            aliases = {len(args) + i: i for i in range(len(buffers))}
            args += buffers
            specs += [any_space()] * len(buffers)
            scratch = [
                pltpu.VMEM((vecs, 2 * padded, width), BF16),
                pltpu.VMEM((2 * vecs * blocks, kind_count * width), BF16),
            ]
            if last:
                outs, out_specs = [full_shape, full_shape], [any_space(), any_space()]
                scratch += [
                    pltpu.VMEM((vecs, blocks, width), F32),
                    pltpu.SemaphoreType.DMA((vecs + 1,)),
                ]
            else:
                outs, out_specs = [chunk_shape, rows, rows], [vmem()] * 3
            outs.append(partial_shape)
            if older:
                outs += [jax.ShapeDtypeStruct((older + 1, groups // 2, quarter, width), F32)] * 2
            out_specs += [vmem()] * (len(outs) - len(out_specs))
            cfg = (
                vecs,
                current[c][1],
                previous[c][1],
                c * vecs,
                last,
                partial is not None,
                older,
                len(buffers),
            )
            result = pl.pallas_call(
                functools.partial(step_kernel, cfg),
                out_shape=outs,
                in_specs=specs,
                out_specs=out_specs,
                scratch_shapes=scratch,
                input_output_aliases=aliases,
                compiler_params=params(),
                cost_estimate=cost(1.5e9, 5e6),
                name=f"step{s}_{c}",
            )(*args)
            if last:
                buffers = list(result[:2])
                partial = result[2]
                rest = result[3:]
            else:
                previous[c], current[c] = current[c], (result[0], 0)
                received[c] = exchange(result[1], result[2])
                partial = result[3]
        partials.append(partial)

    keep, give = rest
    got = lax.ppermute(give, "vec", [(i, i ^ 1) for i in range(groups)])
    piece = jax.ShapeDtypeStruct((STEPS, quarter, width), F32)
    mine, give = pl.pallas_call(
        fold_kernel,
        out_shape=[piece, piece],
        in_specs=[smem(), vmem(), vmem()],
        out_specs=[vmem(), vmem()],
        compiler_params=params(),
        cost_estimate=cost(1e5, 1e6),
        name="fold",
    )(index, keep, got)
    got = lax.ppermute(give, "vec", [(i, i ^ 2) for i in range(groups)])

    prior_count = prior_moments.shape[0]
    moment_count = prior_count + STEPS
    even_table, odd_table = jackson_split(moment_count, ENERGIES)
    group, lanes = 8, 128
    small = pl.BlockSpec((STEPS, group, lanes), lambda i, h: (0, i, h))
    new_moments, energy_map = pl.pallas_call(
        functools.partial(energy_kernel, vec_dev * groups),
        out_shape=[piece, jax.ShapeDtypeStruct((ENERGIES, quarter, width), F32)],
        grid=(quarter // group, width // lanes),
        in_specs=[
            pl.BlockSpec(even_table.shape, lambda i, h: (0, 0)),
            pl.BlockSpec(odd_table.shape, lambda i, h: (0, 0)),
            pl.BlockSpec((prior_count, group, lanes), lambda i, h: (0, i, h)),
            small,
            small,
        ],
        out_specs=[small, pl.BlockSpec((ENERGIES, group, lanes), lambda i, h: (0, i, h))],
        scratch_shapes=[pltpu.VMEM((moment_count * group, lanes), F32)],
        compiler_params=params(),
        cost_estimate=cost(4e9, 2.2e7),
        name="energy",
    )(jnp.asarray(even_table), jnp.asarray(odd_table), prior_moments, mine, got)
    return buffers[0], buffers[1], new_moments, energy_map


def solution(mesh):
    return jax.shard_map(
        per_device,
        mesh=mesh,
        in_specs=(
            P("vec", "dom", None),
            P("vec", "dom", None),
            P("vec", "dom", None),
            P(None, ("dom", "vec"), None),
            P(None, "dom", None),
            P(),
            P("dom", None),
            P("dom", None, None),
            P("dom", None),
        ),
        out_specs=(
            P("vec", "dom", None),
            P("vec", "dom", None),
            P(None, ("dom", "vec"), None),
            P(None, ("dom", "vec"), None),
        ),
        check_vma=False,
    )
```

```python
import functools
import math

import jax
import jax.numpy as jnp
import numpy as np
from jax import lax
from jax.experimental import pallas as pl
from jax.experimental.pallas import tpu as pltpu
from jax.sharding import PartitionSpec as P


ENERGIES = 512
STEPS = 4
F32 = jnp.float32
BF16 = jnp.bfloat16
VMEM_LIMIT = 24 * 1024 * 1024


def split(x):
    high = x.astype(BF16)
    return high, (x - high.astype(F32)).astype(BF16)


def dot(a, b):
    return jnp.dot(a, b, preferred_element_type=F32)


def jackson_split(moment_count, energy_count):
    m = np.arange(moment_count, dtype=np.float64)
    step = math.pi / (moment_count + 1.0)
    damping = (
        (moment_count - m + 1.0) * np.cos(step * m) + np.sin(step * m) / math.tan(step)
    ) / (moment_count + 1.0)
    weights = np.where(m == 0, damping, 2.0 * damping)
    angles = math.pi * (np.arange(energy_count // 2) + 0.5) / energy_count
    table = (weights[None, :] * np.cos(angles[:, None] * m[None, :])).astype(np.float32)
    halves = []
    for parity in range(2):
        part = table[:, parity::2]
        high = part.astype(BF16)
        low = (part - high.astype(np.float32)).astype(BF16)
        halves.append(np.concatenate([high, low, high, low], axis=1))
    return halves


def vmem():
    return pl.BlockSpec(memory_space=pltpu.VMEM)


def smem():
    return pl.BlockSpec(memory_space=pltpu.SMEM)


def params(limit=VMEM_LIMIT):
    return pltpu.CompilerParams(vmem_limit_bytes=limit)


def cost(flops, size):
    return pl.CostEstimate(flops=int(flops), bytes_accessed=int(size), transcendentals=0)


def gather_rows(onehot, value):
    high, low = split(value)
    return dot(onehot, jnp.concatenate([high, low], axis=0))


def any_space():
    return pl.BlockSpec(memory_space=pl.ANY)


def hbm():
    return pl.BlockSpec(memory_space=pltpu.HBM)


def stay(x):
    return pltpu.with_memory_space_constraint(x, pltpu.HBM)


def first_kernel(rim, vecs, index_ref, lists_hbm, cur_hbm, pick_ref, cur_ref, *rest):
    sends, (lists_ref, sems) = rest[:-2], rest[-2:]
    count, blocks, width = cur_ref.shape
    list_copy = pltpu.make_async_copy(lists_hbm, lists_ref, sems.at[count])
    list_copy.start()
    copies = [pltpu.make_async_copy(cur_hbm.at[v], cur_ref.at[v], sems.at[v]) for v in range(count)]
    for copy in copies:
        copy.start()
    list_copy.wait()
    lists = lists_ref[0]
    even = index_ref[0] == 0
    rows = lax.broadcasted_iota(jnp.int32, (rim, rim), 0)
    lanes = lax.broadcasted_iota(jnp.int32, (rim, rim), 1)
    slots = lax.broadcasted_iota(jnp.int32, (rim, blocks), 1)
    for half in range(2):
        mine = lists[half : half + 1]
        other = lists[1 - half : 2 - half]
        chosen = jnp.where(even, mine, other)
        spread = jnp.where(rows == lanes, chosen, 0).astype(F32)
        column = jnp.sum(spread, axis=1, keepdims=True).astype(jnp.int32)
        onehot = jnp.where(slots == column, 1.0, 0.0).astype(BF16)
        pick_ref[pl.ds(half * rim, rim), 0:blocks] = onehot
        pick_ref[pl.ds(half * rim, rim), blocks : 2 * blocks] = onehot
    pick = pick_ref[...]
    for v in range(count):
        chunk, place = divmod(v, vecs)
        copies[v].wait()
        got = gather_rows(pick, cur_ref[v])
        for half in range(2):
            sends[2 * chunk + half][:, place * width : (place + 1) * width] = got[
                half * rim : (half + 1) * rim
            ]


def prep_kernel(
    rim,
    index_ref,
    cols_hbm,
    ids_hbm,
    kinds_hbm,
    prev_hbm,
    probe_hbm,
    site_hbm,
    mix_ref,
    high_ref,
    low_ref,
    prev_ref,
    probe_ref,
    site_ref,
    cols_ref,
    ids_ref,
    kinds,
    sems,
):
    links, blocks = cols_ref.shape
    kind_count, width = kinds.shape[:2]
    padded = mix_ref.shape[1] // 2
    copies = [
        pltpu.make_async_copy(kinds_hbm.at[n], kinds.at[n], sems.at[n]) for n in range(kind_count)
    ]
    fetched = ((prev_hbm, prev_ref), (probe_hbm, probe_ref), (site_hbm, site_ref))
    small = [
        pltpu.make_async_copy(cols_hbm, cols_ref, sems.at[kind_count + 3]),
        pltpu.make_async_copy(ids_hbm, ids_ref, sems.at[kind_count + 4]),
    ]
    for copy in small:
        copy.start()
    for i, (source, target) in enumerate(fetched):
        copies.append(pltpu.make_async_copy(source, target, sems.at[kind_count + i]))
    for copy in copies:
        copy.start()
    even = index_ref[0] == 0
    rows = lax.broadcasted_iota(jnp.int32, (padded, blocks), 0)
    corner = lax.broadcasted_iota(jnp.int32, (blocks, blocks), 0)
    diagonal = corner == lax.broadcasted_iota(jnp.int32, (blocks, blocks), 1)
    identity = jnp.where(diagonal, 1.0, 0.0).astype(BF16)
    for copy in small:
        copy.wait()
    e = cols_ref[...]
    crossed = jnp.where(e < blocks + rim, e + rim, e - rim)
    e = jnp.where(jnp.logical_and(even, e >= blocks), crossed, e)
    ids = ids_ref[...]
    for n in range(kind_count):
        mine = jnp.where(ids == n, e, -1)
        total = jnp.zeros((padded, blocks), F32)
        for k in range(links):
            total += jnp.where(rows == mine[k : k + 1], 1.0, 0.0)
        turned = lax.dot_general(
            identity, total.astype(BF16), (((1,), (1,)), ((), ())), preferred_element_type=F32
        ).astype(BF16)
        mix_ref[n * blocks : (n + 1) * blocks, 0:padded] = turned
        mix_ref[n * blocks : (n + 1) * blocks, padded : 2 * padded] = turned
    for n in range(kind_count):
        copies[n].wait()
        high, low = split(2.0 * kinds[n])
        high_ref[n * width : (n + 1) * width] = high
        low_ref[n * width : (n + 1) * width] = low
    for copy in copies[kind_count:]:
        copy.wait()


def step_kernel(
    cfg,
    index_ref,
    mix_ref,
    high_ref,
    low_ref,
    pick_ref,
    site_ref,
    cur_ref,
    prev_ref,
    probe_ref,
    recv_a,
    recv_b,
    *rest,
):
    vecs, cur_at, prev_at, own_at, last, add_partial, older, fold, aliased = cfg
    rest = list(rest)
    partial_in = rest.pop(0) if add_partial else None
    olders = [rest.pop(0) for _ in range(older)]
    rest = rest[aliased:]
    out_ref, partial_out = rest[:2]
    rest = rest[2:]
    if last:
        prev_out = rest.pop(0)
    else:
        send_a, send_b = rest.pop(0), rest.pop(0)
    if fold:
        keep_ref, give_ref = rest.pop(0), rest.pop(0)
    source, mixed = rest[:2]
    blocks, width = cur_ref.shape[1:]
    rim = recv_a.shape[0]
    padded = source.shape[1] // 2
    kind_count = mix_ref.shape[0] // blocks
    spin = width // 2
    if last:
        copy = pltpu.make_async_copy(
            cur_ref.at[pl.ds(cur_at, vecs)], prev_out.at[pl.ds(own_at, vecs)], rest[2]
        )
        copy.start()
    for v in range(vecs):
        columns = slice(v * width, (v + 1) * width)
        pieces = [cur_ref[cur_at + v], recv_a[:, columns], recv_b[:, columns]]
        used = blocks + 2 * rim
        if used < padded:
            pieces.append(jnp.zeros((padded - used, width), F32))
        high, low = split(jnp.concatenate(pieces, axis=0))
        source[v, 0:padded] = high
        source[v, padded : 2 * padded] = low
    for v in range(vecs):
        mixture = dot(mix_ref[...], source[v])
        high, low = split(mixture)
        for n in range(kind_count):
            columns = slice(n * width, (n + 1) * width)
            rows = slice(n * blocks, (n + 1) * blocks)
            mixed[v * blocks : (v + 1) * blocks, columns] = high[rows]
            mixed[(vecs + v) * blocks : (vecs + v + 1) * blocks, columns] = low[rows]
    count = vecs * blocks
    both = dot(mixed[...], high_ref[...])
    hopping = both[:count] + both[count:] + dot(mixed[:count], low_ref[...])
    diag_up = 2.0 * (site_ref[0] + site_ref[1])
    diag_down = 2.0 * (site_ref[0] - site_ref[1])
    cross = 2.0 * site_ref[2]
    partial = partial_in[...] if add_partial else None
    for v in range(vecs):
        here = cur_ref[cur_at + v]
        up = here[:, :spin]
        down = here[:, spin:]
        onsite = jnp.concatenate(
            [diag_up * up + cross * down, diag_down * down + cross * up], axis=1
        )
        following = hopping[v * blocks : (v + 1) * blocks] + onsite - prev_ref[prev_at + v]
        out_ref[v] = following
        term = probe_ref[own_at + v] * following
        partial = term if partial is None else partial + term
        if not last:
            got = gather_rows(pick_ref[...], following)
            send_a[:, v * width : (v + 1) * width] = got[:rim]
            send_b[:, v * width : (v + 1) * width] = got[rim:]
    partial_out[...] = partial
    if fold:
        cores = 2
        quarter = keep_ref.shape[2]
        core = index_ref[1]
        for s in range(older + 1):
            ref = olders[s] if s < older else partial_out
            for y in range(keep_ref.shape[1]):
                base = y * cores * quarter
                keep_ref[s, y] = ref[pl.ds(pl.multiple_of(base + core * quarter, quarter), quarter)]
                give_ref[s, y] = ref[
                    pl.ds(pl.multiple_of(base + (1 - core) * quarter, quarter), quarter)
                ]
    if last:
        copy.wait()


def fold_kernel(index_ref, keep_ref, got_ref, mine_ref, give_ref):
    y = index_ref[2]
    mine_ref[...] = keep_ref[:, y] + got_ref[:, y]
    give_ref[...] = keep_ref[:, 1 - y] + got_ref[:, 1 - y]


def energy_kernel(
    vector_total,
    chunks,
    even_ref,
    odd_ref,
    prior_ref,
    early_mine,
    early_got,
    late_mine,
    late_got,
    *rest,
):
    finals = rest[:chunks]
    new_ref, map_ref, cur_out, moments, sems = rest[chunks:]
    vecs = finals[0].shape[0]
    copies = [
        pltpu.make_async_copy(finals[c], cur_out.at[pl.ds(c * vecs, vecs)], sems.at[c])
        for c in range(chunks)
    ]
    step = pl.program_id(0) * pl.num_programs(1) + pl.program_id(1)

    @pl.when(step == 0)
    def _():
        for copy in copies:
            copy.start()

    prior_count, group, lanes = prior_ref.shape
    early, late = early_mine.shape[0], late_mine.shape[0]
    steps = early + late
    half = even_ref.shape[0]
    pairs = (prior_count + steps) // 2
    new_ref[0:early] = (early_mine[...] + early_got[...]) * (1.0 / vector_total)
    new_ref[early:steps] = (late_mine[...] + late_got[...]) * (1.0 / vector_total)
    moments[0 : prior_count * group] = prior_ref[...].reshape(prior_count * group, lanes)
    moments[prior_count * group :] = new_ref[...].reshape(steps * group, lanes)
    flat = map_ref.reshape(2 * half * group, lanes)
    flip = 7 - lax.broadcasted_iota(jnp.int32, (8, lanes), 0)
    for b in range(0, group, 2):
        sums = []
        for parity, table in ((0, even_ref), (1, odd_ref)):
            pair = [
                moments[pl.ds(parity * group + b + i, pairs, stride=2 * group)] for i in range(2)
            ]
            high, low = split(jnp.concatenate(pair, axis=1))
            sums.append(dot(table[...], jnp.concatenate([high, high, low, low], axis=0)))
        plus = sums[0] + sums[1]
        minus = sums[0] - sums[1]
        for i in range(2):
            columns = slice(i * lanes, (i + 1) * lanes)
            flat[pl.ds(b + i, half, stride=group)] = plus[:, columns]
            for r in range(0, half, 8):
                turned = jnp.take_along_axis(minus[r : r + 8, columns], flip, axis=0)
                top = 2 * half - 8 - r
                flat[pl.ds(top * group + b + i, 8, stride=group)] = turned

    @pl.when(step == pl.num_programs(0) * pl.num_programs(1) - 1)
    def _():
        for copy in copies:
            copy.wait()


def per_device(
    probe,
    cheb_prev,
    cheb_cur,
    prior_moments,
    site_terms,
    hop_kinds,
    tile_kind_ids,
    send_lists,
    tile_cols,
):
    vec_dev, blocks, width = cheb_cur.shape
    kind_count = hop_kinds.shape[0]
    groups = lax.axis_size("vec")
    domains = lax.axis_size("dom")
    rim = send_lists.shape[2]
    chunks = 2
    vecs = vec_dev // chunks
    quarter = blocks // groups
    padded = -(-(blocks + 2 * rim) // 256) * 256
    swap_a = [(i, i ^ 1) for i in range(domains)]
    swap_b = [(i, (i + 1) % domains if i % 2 else (i - 1) % domains) for i in range(domains)]
    vec_index = lax.axis_index("vec")
    index = jnp.stack([lax.axis_index("dom") % 2, vec_index % 2, vec_index // 2]).astype(jnp.int32)

    rows = jax.ShapeDtypeStruct((rim, vecs * width), F32)
    full_shape = jax.ShapeDtypeStruct((vec_dev, blocks, width), F32)
    chunk_shape = jax.ShapeDtypeStruct((vecs, blocks, width), F32)
    first = pl.pallas_call(
        functools.partial(first_kernel, rim, vecs),
        out_shape=[jax.ShapeDtypeStruct((2 * rim, 2 * blocks), BF16), full_shape]
        + [rows] * (2 * chunks),
        in_specs=[smem(), hbm(), hbm()],
        out_specs=[vmem()] * (2 + 2 * chunks),
        scratch_shapes=[
            pltpu.VMEM(send_lists.shape, jnp.int32),
            pltpu.SemaphoreType.DMA((vec_dev + 1,)),
        ],
        compiler_params=params(),
        cost_estimate=cost(1e8, 1e6),
        name="first_sends",
    )(index, stay(send_lists), stay(cheb_cur))
    pick, cur_held, sends = first[0], first[1], list(first[2:])

    def exchange(a, b):
        got_b = lax.ppermute(b, "dom", swap_b)
        got_a = lax.ppermute(a, "dom", swap_a)
        return got_a, got_b

    received = [exchange(sends[2 * c], sends[2 * c + 1]) for c in range(chunks)]

    mix, high, low, prev_held, probe_held, site_held = pl.pallas_call(
        functools.partial(prep_kernel, rim),
        out_shape=[
            jax.ShapeDtypeStruct((kind_count * blocks, 2 * padded), BF16),
            jax.ShapeDtypeStruct((kind_count * width, width), BF16),
            jax.ShapeDtypeStruct((kind_count * width, width), BF16),
            full_shape,
            full_shape,
            jax.ShapeDtypeStruct(site_terms.shape, F32),
        ],
        in_specs=[smem()] + [hbm()] * 6,
        out_specs=[vmem()] * 6,
        scratch_shapes=[
            pltpu.VMEM(tile_cols.shape[::-1], jnp.int32),
            pltpu.VMEM(tile_cols.shape[::-1], jnp.int32),
            pltpu.VMEM(hop_kinds.shape, F32),
            pltpu.SemaphoreType.DMA((kind_count + 5,)),
        ],
        compiler_params=params(),
        cost_estimate=cost(1e7, 8e6),
        name="tables",
    )(
        index,
        *[
            stay(x)
            for x in (tile_cols.T, tile_kind_ids.T, hop_kinds, cheb_prev, probe, site_terms)
        ],
    )

    partial_shape = jax.ShapeDtypeStruct((blocks, width), F32)
    current = [(cur_held, c * vecs) for c in range(chunks)]
    previous = [(prev_held, c * vecs) for c in range(chunks)]

    def reduce(keep, give):
        got = lax.ppermute(give, "vec", [(i, i ^ 1) for i in range(groups)])
        piece = jax.ShapeDtypeStruct((keep.shape[0], quarter, width), F32)
        mine, give = pl.pallas_call(
            fold_kernel,
            out_shape=[piece, piece],
            in_specs=[smem(), vmem(), vmem()],
            out_specs=[vmem(), vmem()],
            compiler_params=params(),
            cost_estimate=cost(1e5, 1e6),
            name="fold",
        )(index, keep, got)
        return mine, lax.ppermute(give, "vec", [(i, i ^ 2) for i in range(groups)])

    partials = []
    buffers = []
    reduced = []
    for s in range(STEPS):
        last = s == STEPS - 1
        partial = None
        for c in range(chunks):
            args = [index, mix, high, low, pick, site_held]
            args += [current[c][0], previous[c][0], probe_held, *received[c]]
            specs = [smem()] + [vmem()] * (len(args) - 1)
            fold = c == chunks - 1 and s >= STEPS - 2
            older = len(partials) if fold else 0
            extra = ([] if partial is None else [partial]) + (partials if fold else [])
            args += extra
            specs += [vmem()] * len(extra)
            aliases = {len(args) + i: 2 + i for i in range(len(buffers))}
            args += buffers
            specs += [any_space()] * len(buffers)
            scratch = [
                pltpu.VMEM((vecs, 2 * padded, width), BF16),
                pltpu.VMEM((2 * vecs * blocks, kind_count * width), BF16),
            ]
            outs, out_specs = [chunk_shape, partial_shape], [vmem(), vmem()]
            if last:
                outs.append(full_shape)
                out_specs.append(any_space())
                scratch.append(pltpu.SemaphoreType.DMA)
            else:
                outs += [rows, rows]
            if fold:
                outs += [jax.ShapeDtypeStruct((older + 1, groups // 2, quarter, width), F32)] * 2
            out_specs += [vmem()] * (len(outs) - len(out_specs))
            cfg = (
                vecs,
                current[c][1],
                previous[c][1],
                c * vecs,
                last,
                partial is not None,
                older,
                fold,
                len(buffers),
            )
            result = list(
                pl.pallas_call(
                    functools.partial(step_kernel, cfg),
                    out_shape=outs,
                    in_specs=specs,
                    out_specs=out_specs,
                    scratch_shapes=scratch,
                    input_output_aliases=aliases,
                    compiler_params=params(),
                    cost_estimate=cost(1.5e9, 5e6),
                )(*args)
            )
            previous[c], current[c] = current[c], (result.pop(0), 0)
            partial = result.pop(0)
            if last:
                buffers = [result.pop(0)]
            else:
                received[c] = exchange(result.pop(0), result.pop(0))
            if fold:
                reduced.append(reduce(*result))
        partials.append(partial)
        if fold:
            partials = []

    prior_count = prior_moments.shape[0]
    moment_count = prior_count + STEPS
    even_table, odd_table = jackson_split(moment_count, ENERGIES)
    group, lanes = 8, 128

    def small(count):
        return pl.BlockSpec((count, group, lanes), lambda i, h: (0, i, h))

    terms = [x for pair in reduced for x in pair]
    new_moments, energy_map, next_cur = pl.pallas_call(
        functools.partial(energy_kernel, vec_dev * groups, chunks),
        out_shape=[
            jax.ShapeDtypeStruct((STEPS, quarter, width), F32),
            jax.ShapeDtypeStruct((ENERGIES, quarter, width), F32),
            full_shape,
        ],
        grid=(quarter // group, width // lanes),
        in_specs=[
            pl.BlockSpec(even_table.shape, lambda i, h: (0, 0)),
            pl.BlockSpec(odd_table.shape, lambda i, h: (0, 0)),
            pl.BlockSpec((prior_count, group, lanes), lambda i, h: (0, i, h)),
            *[small(x.shape[0]) for x in terms],
            *[vmem()] * chunks,
        ],
        out_specs=[
            small(STEPS),
            pl.BlockSpec((ENERGIES, group, lanes), lambda i, h: (0, i, h)),
            any_space(),
        ],
        scratch_shapes=[
            pltpu.VMEM((moment_count * group, lanes), F32),
            pltpu.SemaphoreType.DMA((chunks,)),
        ],
        compiler_params=params(),
        cost_estimate=cost(4e9, 2.2e7),
        name="energy",
    )(
        jnp.asarray(even_table),
        jnp.asarray(odd_table),
        prior_moments,
        *terms,
        *[current[c][0] for c in range(chunks)],
    )
    return buffers[0], next_cur, new_moments, energy_map


def solution(mesh):
    return jax.shard_map(
        per_device,
        mesh=mesh,
        in_specs=(
            P("vec", "dom", None),
            P("vec", "dom", None),
            P("vec", "dom", None),
            P(None, ("dom", "vec"), None),
            P(None, "dom", None),
            P(),
            P("dom", None),
            P("dom", None, None),
            P("dom", None),
        ),
        out_specs=(
            P("vec", "dom", None),
            P("vec", "dom", None),
            P(None, ("dom", "vec"), None),
            P(None, ("dom", "vec"), None),
        ),
        check_vma=False,
    )
```

```python
import functools
import math

import jax
import jax.numpy as jnp
import numpy as np
from jax import lax
from jax.experimental import pallas as pl
from jax.experimental.pallas import tpu as pltpu
from jax.sharding import PartitionSpec as P


ENERGIES = 512
STEPS = 4
F32 = jnp.float32
BF16 = jnp.bfloat16
VMEM_LIMIT = 24 * 1024 * 1024


def split(x):
    high = x.astype(BF16)
    return high, (x - high.astype(F32)).astype(BF16)


def dot(a, b):
    return jnp.dot(a, b, preferred_element_type=F32)


def jackson_split(moment_count, energy_count):
    m = np.arange(moment_count, dtype=np.float64)
    step = math.pi / (moment_count + 1.0)
    damping = (
        (moment_count - m + 1.0) * np.cos(step * m) + np.sin(step * m) / math.tan(step)
    ) / (moment_count + 1.0)
    weights = np.where(m == 0, damping, 2.0 * damping)
    angles = math.pi * (np.arange(energy_count // 2) + 0.5) / energy_count
    table = (weights[None, :] * np.cos(angles[:, None] * m[None, :])).astype(np.float32)
    halves = []
    for parity in range(2):
        part = table[:, parity::2]
        high = part.astype(BF16)
        low = (part - high.astype(np.float32)).astype(BF16)
        halves.append(np.concatenate([high, low, high, low], axis=1))
    return halves


def vmem():
    return pl.BlockSpec(memory_space=pltpu.VMEM)


def smem():
    return pl.BlockSpec(memory_space=pltpu.SMEM)


def params(limit=VMEM_LIMIT):
    return pltpu.CompilerParams(vmem_limit_bytes=limit)


def cost(flops, size):
    return pl.CostEstimate(flops=int(flops), bytes_accessed=int(size), transcendentals=0)


def gather_rows(onehot, value):
    high, low = split(value)
    return dot(onehot, jnp.concatenate([high, low], axis=0))


def any_space():
    return pl.BlockSpec(memory_space=pl.ANY)


def hbm():
    return pl.BlockSpec(memory_space=pltpu.HBM)


def stay(x):
    return pltpu.with_memory_space_constraint(x, pltpu.HBM)


def first_kernel(rim, vecs, index_ref, lists_hbm, cur_hbm, pick_ref, cur_ref, *rest):
    sends, (lists_ref, sems) = rest[:-2], rest[-2:]
    count, blocks, width = cur_ref.shape
    list_copy = pltpu.make_async_copy(lists_hbm, lists_ref, sems.at[count])
    list_copy.start()
    copies = [pltpu.make_async_copy(cur_hbm.at[v], cur_ref.at[v], sems.at[v]) for v in range(count)]
    for copy in copies:
        copy.start()
    list_copy.wait()
    lists = lists_ref[0]
    even = index_ref[0] == 0
    rows = lax.broadcasted_iota(jnp.int32, (rim, rim), 0)
    lanes = lax.broadcasted_iota(jnp.int32, (rim, rim), 1)
    slots = lax.broadcasted_iota(jnp.int32, (rim, blocks), 1)
    for half in range(2):
        mine = lists[half : half + 1]
        other = lists[1 - half : 2 - half]
        chosen = jnp.where(even, mine, other)
        spread = jnp.where(rows == lanes, chosen, 0).astype(F32)
        column = jnp.sum(spread, axis=1, keepdims=True).astype(jnp.int32)
        onehot = jnp.where(slots == column, 1.0, 0.0).astype(BF16)
        pick_ref[pl.ds(half * rim, rim), 0:blocks] = onehot
        pick_ref[pl.ds(half * rim, rim), blocks : 2 * blocks] = onehot
    pick = pick_ref[...]
    for v in range(count):
        chunk, place = divmod(v, vecs)
        copies[v].wait()
        got = gather_rows(pick, cur_ref[v])
        for half in range(2):
            sends[2 * chunk + half][:, place * width : (place + 1) * width] = got[
                half * rim : (half + 1) * rim
            ]


def prep_kernel(
    rim,
    index_ref,
    cols_hbm,
    ids_hbm,
    kinds_hbm,
    prev_hbm,
    probe_hbm,
    site_hbm,
    mix_ref,
    high_ref,
    low_ref,
    prev_ref,
    probe_ref,
    site_ref,
    cols_ref,
    ids_ref,
    kinds,
    sems,
):
    links, blocks = cols_ref.shape
    kind_count, width = kinds.shape[:2]
    padded = mix_ref.shape[1] // 2
    copies = [
        pltpu.make_async_copy(kinds_hbm.at[n], kinds.at[n], sems.at[n]) for n in range(kind_count)
    ]
    fetched = ((prev_hbm, prev_ref), (probe_hbm, probe_ref), (site_hbm, site_ref))
    small = [
        pltpu.make_async_copy(cols_hbm, cols_ref, sems.at[kind_count + 3]),
        pltpu.make_async_copy(ids_hbm, ids_ref, sems.at[kind_count + 4]),
    ]
    for copy in small:
        copy.start()
    for i, (source, target) in enumerate(fetched):
        copies.append(pltpu.make_async_copy(source, target, sems.at[kind_count + i]))
    for copy in copies:
        copy.start()
    even = index_ref[0] == 0
    rows = lax.broadcasted_iota(jnp.int32, (padded, blocks), 0)
    corner = lax.broadcasted_iota(jnp.int32, (blocks, blocks), 0)
    diagonal = corner == lax.broadcasted_iota(jnp.int32, (blocks, blocks), 1)
    identity = jnp.where(diagonal, 1.0, 0.0).astype(BF16)
    for copy in small:
        copy.wait()
    e = cols_ref[...]
    crossed = jnp.where(e < blocks + rim, e + rim, e - rim)
    e = jnp.where(jnp.logical_and(even, e >= blocks), crossed, e)
    ids = ids_ref[...]
    for n in range(kind_count):
        mine = jnp.where(ids == n, e, -1)
        total = jnp.zeros((padded, blocks), F32)
        for k in range(links):
            total += jnp.where(rows == mine[k : k + 1], 1.0, 0.0)
        turned = lax.dot_general(
            identity, total.astype(BF16), (((1,), (1,)), ((), ())), preferred_element_type=F32
        ).astype(BF16)
        mix_ref[n * blocks : (n + 1) * blocks, 0:padded] = turned
        mix_ref[n * blocks : (n + 1) * blocks, padded : 2 * padded] = turned
    for n in range(kind_count):
        copies[n].wait()
        high, low = split(2.0 * kinds[n])
        high_ref[n * width : (n + 1) * width] = high
        low_ref[n * width : (n + 1) * width] = low
    for copy in copies[kind_count:]:
        copy.wait()


def step_kernel(
    cfg,
    index_ref,
    mix_ref,
    high_ref,
    low_ref,
    pick_ref,
    site_ref,
    cur_ref,
    prev_ref,
    probe_ref,
    recv_a,
    recv_b,
    *rest,
):
    vecs, cur_at, prev_at, own_at, last, add_partial, older, fold, fetch, aliased = cfg
    rest = list(rest)
    partial_in = rest.pop(0) if add_partial else None
    olders = [rest.pop(0) for _ in range(older)]
    prior_hbm = rest.pop(0) if fetch else None
    rest = rest[aliased:]
    out_ref, partial_out = rest[:2]
    rest = rest[2:]
    if last:
        prev_out = rest.pop(0)
    else:
        send_a, send_b = rest.pop(0), rest.pop(0)
    if fold and last:
        pieces_out = [rest.pop(0) for _ in range(4)]
    elif fold:
        keep_ref, give_ref = rest.pop(0), rest.pop(0)
    if fetch:
        prior_ref = rest.pop(0)
    source, mixed = rest[:2]
    blocks, width = cur_ref.shape[1:]
    rim = recv_a.shape[0]
    padded = source.shape[1] // 2
    kind_count = mix_ref.shape[0] // blocks
    spin = width // 2
    copies = []
    if last:
        copies = [
            pltpu.make_async_copy(
                cur_ref.at[pl.ds(cur_at, vecs)], prev_out.at[pl.ds(own_at, vecs)], rest[2]
            )
        ]
    if fetch:
        count, halves, moments, group, lanes = prior_ref.shape
        known = prior_hbm.shape[0]
        copies = [
            pltpu.make_async_copy(
                prior_hbm.at[:, pl.ds(i * group, group), pl.ds(h * lanes, lanes)],
                prior_ref.at[i, h, pl.ds(0, known)],
                rest[2].at[i * halves + h],
            )
            for i in range(count)
            for h in range(halves)
        ]
    for copy in copies:
        copy.start()
    if fetch:
        prior_ref[:, :, known:] = jnp.zeros((count, halves, moments - known, group, lanes), F32)
    for v in range(vecs):
        columns = slice(v * width, (v + 1) * width)
        pieces = [cur_ref[cur_at + v], recv_a[:, columns], recv_b[:, columns]]
        used = blocks + 2 * rim
        if used < padded:
            pieces.append(jnp.zeros((padded - used, width), F32))
        high, low = split(jnp.concatenate(pieces, axis=0))
        source[v, 0:padded] = high
        source[v, padded : 2 * padded] = low
    for v in range(vecs):
        mixture = dot(mix_ref[...], source[v])
        high, low = split(mixture)
        for n in range(kind_count):
            columns = slice(n * width, (n + 1) * width)
            rows = slice(n * blocks, (n + 1) * blocks)
            mixed[v * blocks : (v + 1) * blocks, columns] = high[rows]
            mixed[(vecs + v) * blocks : (vecs + v + 1) * blocks, columns] = low[rows]
    count = vecs * blocks
    both = dot(mixed[...], high_ref[...])
    hopping = both[:count] + both[count:] + dot(mixed[:count], low_ref[...])
    diag_up = 2.0 * (site_ref[0] + site_ref[1])
    diag_down = 2.0 * (site_ref[0] - site_ref[1])
    cross = 2.0 * site_ref[2]
    partial = partial_in[...] if add_partial else None
    for v in range(vecs):
        here = cur_ref[cur_at + v]
        up = here[:, :spin]
        down = here[:, spin:]
        onsite = jnp.concatenate(
            [diag_up * up + cross * down, diag_down * down + cross * up], axis=1
        )
        following = hopping[v * blocks : (v + 1) * blocks] + onsite - prev_ref[prev_at + v]
        out_ref[v] = following
        term = probe_ref[own_at + v] * following
        partial = term if partial is None else partial + term
        if not last:
            got = gather_rows(pick_ref[...], following)
            send_a[:, v * width : (v + 1) * width] = got[:rim]
            send_b[:, v * width : (v + 1) * width] = got[rim:]
    partial_out[...] = partial
    if fold and last:
        quarter = pieces_out[0].shape[0]
        for flip, piece in enumerate(pieces_out):
            core = index_ref[1] if flip % 2 == 0 else 1 - index_ref[1]
            chip = index_ref[2] if flip < 2 else 1 - index_ref[2]
            at = pl.multiple_of((2 * chip + core) * quarter, quarter)
            piece[...] = partial_out[pl.ds(at, quarter)]
    elif fold:
        cores = 2
        quarter = keep_ref.shape[2]
        core = index_ref[1]
        for s in range(older + 1):
            ref = olders[s] if s < older else partial_out
            for y in range(keep_ref.shape[1]):
                base = y * cores * quarter
                keep_ref[s, y] = ref[pl.ds(pl.multiple_of(base + core * quarter, quarter), quarter)]
                give_ref[s, y] = ref[
                    pl.ds(pl.multiple_of(base + (1 - core) * quarter, quarter), quarter)
                ]
    for copy in copies:
        copy.wait()


def fold_kernel(index_ref, keep_ref, got_ref, mine_ref, give_ref):
    y = index_ref[2]
    mine_ref[...] = keep_ref[:, y] + got_ref[:, y]
    give_ref[...] = keep_ref[:, 1 - y] + got_ref[:, 1 - y]


def energy_kernel(vector_total, chunks, even_ref, odd_ref, prior_ref, early_mine, early_got, *rest):
    lates, finals = rest[:4], rest[4 : 4 + chunks]
    new_ref, map_out, cur_out, fresh, held, sems = rest[4 + chunks :]
    count, halves, moments, group, lanes = prior_ref.shape
    vecs = finals[0].shape[0]
    copies = [
        pltpu.make_async_copy(
            finals[c], cur_out.at[pl.ds(c * vecs, vecs)], sems.at[count * halves + c]
        )
        for c in range(chunks)
    ]
    for copy in copies:
        copy.start()
    early = early_mine.shape[0]
    steps = new_ref.shape[0]
    scale = 1.0 / vector_total
    new_ref[0:early] = (early_mine[...] + early_got[...]) * scale
    new_ref[early] = ((lates[0][...] + lates[1][...]) + (lates[2][...] + lates[3][...])) * scale
    half = even_ref.shape[0]
    pairs = moments // 2
    flip = 7 - lax.broadcasted_iota(jnp.int32, (8, lanes), 0)
    for i in range(count):
        for h in range(halves):
            slot = i * halves + h
            rows = slice(i * group, (i + 1) * group)
            columns = slice(h * lanes, (h + 1) * lanes)
            old = prior_ref.at[i, h].reshape(moments * group, lanes)
            tail = (8 * 2 - steps) * group
            fresh[slot, 0:tail] = jnp.zeros((tail, lanes), F32)
            fresh[slot, tail:] = new_ref[:, rows, columns].reshape(steps * group, lanes)
            flat = held.at[slot].reshape(2 * half * group, lanes)
            for b in range(0, group, 2):
                sums = []
                for parity, table in ((0, even_ref), (1, odd_ref)):
                    pair = []
                    for j in range(2):
                        start = parity * group + b + j
                        value = old[pl.ds(start, pairs, stride=2 * group)]
                        added = fresh[slot, pl.ds(start, 8, stride=2 * group)]
                        pair.append(
                            jnp.concatenate([value[: pairs - 8], value[pairs - 8 :] + added], axis=0)
                        )
                    high, low = split(jnp.concatenate(pair, axis=1))
                    sums.append(dot(table[...], jnp.concatenate([high, high, low, low], axis=0)))
                plus = sums[0] + sums[1]
                minus = sums[0] - sums[1]
                for j in range(2):
                    side = slice(j * lanes, (j + 1) * lanes)
                    flat[pl.ds(b + j, half, stride=group)] = plus[:, side]
                    for r in range(0, half, 8):
                        turned = jnp.take_along_axis(minus[r : r + 8, side], flip, axis=0)
                        top = 2 * half - 8 - r
                        flat[pl.ds(top * group + b + j, 8, stride=group)] = turned
            copy = pltpu.make_async_copy(
                held.at[slot],
                map_out.at[:, pl.ds(i * group, group), pl.ds(h * lanes, lanes)],
                sems.at[slot],
            )
            copy.start()
            copies.append(copy)
    for copy in copies:
        copy.wait()


def per_device(
    probe,
    cheb_prev,
    cheb_cur,
    prior_moments,
    site_terms,
    hop_kinds,
    tile_kind_ids,
    send_lists,
    tile_cols,
):
    group, lanes = 8, 128
    moment_count = prior_moments.shape[0] + STEPS
    vec_dev, blocks, width = cheb_cur.shape
    kind_count = hop_kinds.shape[0]
    groups = lax.axis_size("vec")
    domains = lax.axis_size("dom")
    rim = send_lists.shape[2]
    chunks = 2
    vecs = vec_dev // chunks
    quarter = blocks // groups
    padded = -(-(blocks + 2 * rim) // 256) * 256
    swap_a = [(i, i ^ 1) for i in range(domains)]
    swap_b = [(i, (i + 1) % domains if i % 2 else (i - 1) % domains) for i in range(domains)]
    vec_index = lax.axis_index("vec")
    index = jnp.stack([lax.axis_index("dom") % 2, vec_index % 2, vec_index // 2]).astype(jnp.int32)

    rows = jax.ShapeDtypeStruct((rim, vecs * width), F32)
    full_shape = jax.ShapeDtypeStruct((vec_dev, blocks, width), F32)
    chunk_shape = jax.ShapeDtypeStruct((vecs, blocks, width), F32)
    first = pl.pallas_call(
        functools.partial(first_kernel, rim, vecs),
        out_shape=[jax.ShapeDtypeStruct((2 * rim, 2 * blocks), BF16), full_shape]
        + [rows] * (2 * chunks),
        in_specs=[smem(), hbm(), hbm()],
        out_specs=[vmem()] * (2 + 2 * chunks),
        scratch_shapes=[
            pltpu.VMEM(send_lists.shape, jnp.int32),
            pltpu.SemaphoreType.DMA((vec_dev + 1,)),
        ],
        compiler_params=params(),
        cost_estimate=cost(1e8, 1e6),
        name="first_sends",
    )(index, stay(send_lists), stay(cheb_cur))
    pick, cur_held, sends = first[0], first[1], list(first[2:])

    def exchange(a, b):
        got_b = lax.ppermute(b, "dom", swap_b)
        got_a = lax.ppermute(a, "dom", swap_a)
        return got_a, got_b

    received = [exchange(sends[2 * c], sends[2 * c + 1]) for c in range(chunks)]

    mix, high, low, prev_held, probe_held, site_held = pl.pallas_call(
        functools.partial(prep_kernel, rim),
        out_shape=[
            jax.ShapeDtypeStruct((kind_count * blocks, 2 * padded), BF16),
            jax.ShapeDtypeStruct((kind_count * width, width), BF16),
            jax.ShapeDtypeStruct((kind_count * width, width), BF16),
            full_shape,
            full_shape,
            jax.ShapeDtypeStruct(site_terms.shape, F32),
        ],
        in_specs=[smem()] + [hbm()] * 6,
        out_specs=[vmem()] * 6,
        scratch_shapes=[
            pltpu.VMEM(tile_cols.shape[::-1], jnp.int32),
            pltpu.VMEM(tile_cols.shape[::-1], jnp.int32),
            pltpu.VMEM(hop_kinds.shape, F32),
            pltpu.SemaphoreType.DMA((kind_count + 5,)),
        ],
        compiler_params=params(),
        cost_estimate=cost(1e7, 8e6),
        name="tables",
    )(
        index,
        *[
            stay(x)
            for x in (tile_cols.T, tile_kind_ids.T, hop_kinds, cheb_prev, probe, site_terms)
        ],
    )

    partial_shape = jax.ShapeDtypeStruct((blocks, width), F32)
    current = [(cur_held, c * vecs) for c in range(chunks)]
    previous = [(prev_held, c * vecs) for c in range(chunks)]

    def reduce(keep, give):
        got = lax.ppermute(give, "vec", [(i, i ^ 1) for i in range(groups)])
        piece = jax.ShapeDtypeStruct((keep.shape[0], quarter, width), F32)
        mine, give = pl.pallas_call(
            fold_kernel,
            out_shape=[piece, piece],
            in_specs=[smem(), vmem(), vmem()],
            out_specs=[vmem(), vmem()],
            compiler_params=params(),
            cost_estimate=cost(1e5, 1e6),
            name="fold",
        )(index, keep, got)
        return mine, lax.ppermute(give, "vec", [(i, i ^ 2) for i in range(groups)])

    partials = []
    buffers = []
    for s in range(STEPS):
        last = s == STEPS - 1
        partial = None
        for c in range(chunks):
            args = [index, mix, high, low, pick, site_held]
            args += [current[c][0], previous[c][0], probe_held, *received[c]]
            specs = [smem()] + [vmem()] * (len(args) - 1)
            fold = c == chunks - 1 and s >= STEPS - 2
            older = 0 if last or not fold else len(partials)
            extra = ([] if partial is None else [partial]) + partials[:older]
            args += extra
            specs += [vmem()] * len(extra)
            fetch = s == STEPS - 2 and c == 0
            if fetch:
                args.append(stay(prior_moments))
                specs.append(hbm())
            aliases = {len(args) + i: 2 + i for i in range(len(buffers))}
            args += buffers
            specs += [any_space()] * len(buffers)
            scratch = [
                pltpu.VMEM((vecs, 2 * padded, width), BF16),
                pltpu.VMEM((2 * vecs * blocks, kind_count * width), BF16),
            ]
            outs, out_specs = [chunk_shape, partial_shape], [vmem(), vmem()]
            if last:
                outs.append(full_shape)
                out_specs.append(any_space())
                scratch.append(pltpu.SemaphoreType.DMA)
            else:
                outs += [rows, rows]
            if fold and last:
                outs += [jax.ShapeDtypeStruct((quarter, width), F32)] * 4
            elif fold:
                outs += [jax.ShapeDtypeStruct((older + 1, groups // 2, quarter, width), F32)] * 2
            if fetch:
                outs.append(
                    jax.ShapeDtypeStruct(
                        (quarter // group, width // lanes, moment_count, group, lanes), F32
                    )
                )
                scratch.append(pltpu.SemaphoreType.DMA((quarter // group * (width // lanes),)))
            out_specs += [vmem()] * (len(outs) - len(out_specs))
            cfg = (
                vecs,
                current[c][1],
                previous[c][1],
                c * vecs,
                last,
                partial is not None,
                older,
                fold,
                fetch,
                len(buffers),
            )
            result = list(
                pl.pallas_call(
                    functools.partial(step_kernel, cfg),
                    out_shape=outs,
                    in_specs=specs,
                    out_specs=out_specs,
                    scratch_shapes=scratch,
                    input_output_aliases=aliases,
                    compiler_params=params(),
                    cost_estimate=cost(1.5e9, 5e6),
                )(*args)
            )
            previous[c], current[c] = current[c], (result.pop(0), 0)
            partial = result.pop(0)
            if last:
                buffers = [result.pop(0)]
            else:
                received[c] = exchange(result.pop(0), result.pop(0))
            if fetch:
                prior_held = result.pop(0)
            if fold and last:
                lates = [result[0]]
                for flip in (2, 3, 1):
                    pairs = [(i, i ^ flip) for i in range(groups)]
                    lates.append(lax.ppermute(result[flip], "vec", pairs))
            elif fold:
                early = reduce(*result)
        partials.append(partial)

    tables = [jnp.asarray(x) for x in jackson_split(moment_count, ENERGIES)]
    tiles = quarter // group * (width // lanes)
    args = [*tables, prior_held, *early, *lates, *[current[c][0] for c in range(chunks)]]
    new_moments, energy_map, next_cur = pl.pallas_call(
        functools.partial(energy_kernel, vec_dev * groups, chunks),
        out_shape=[
            jax.ShapeDtypeStruct((STEPS, quarter, width), F32),
            jax.ShapeDtypeStruct((ENERGIES, quarter, width), F32),
            full_shape,
        ],
        in_specs=[vmem()] * len(args),
        out_specs=[vmem(), any_space(), any_space()],
        scratch_shapes=[
            pltpu.VMEM((tiles, 16 * group, lanes), F32),
            pltpu.VMEM((tiles, ENERGIES, group, lanes), F32),
            pltpu.SemaphoreType.DMA((tiles + chunks,)),
        ],
        compiler_params=params(),
        cost_estimate=cost(4e9, 2.2e7),
        name="energy",
    )(*args)
    return buffers[0], next_cur, new_moments, energy_map


def solution(mesh):
    return jax.shard_map(
        per_device,
        mesh=mesh,
        in_specs=(
            P("vec", "dom", None),
            P("vec", "dom", None),
            P("vec", "dom", None),
            P(None, ("dom", "vec"), None),
            P(None, "dom", None),
            P(),
            P("dom", None),
            P("dom", None, None),
            P("dom", None),
        ),
        out_specs=(
            P("vec", "dom", None),
            P("vec", "dom", None),
            P(None, ("dom", "vec"), None),
            P(None, ("dom", "vec"), None),
        ),
        check_vma=False,
    )
```

```python
import functools
import math

import jax
import jax.numpy as jnp
import numpy as np
from jax import lax
from jax.experimental import pallas as pl
from jax.experimental.pallas import tpu as pltpu
from jax.sharding import PartitionSpec as P


ENERGIES = 512
STEPS = 4
F32 = jnp.float32
BF16 = jnp.bfloat16
VMEM_LIMIT = 24 * 1024 * 1024


def split(x):
    high = x.astype(BF16)
    return high, (x - high.astype(F32)).astype(BF16)


def dot(a, b):
    return jnp.dot(a, b, preferred_element_type=F32)


def jackson_split(moment_count, energy_count):
    m = np.arange(moment_count, dtype=np.float64)
    step = math.pi / (moment_count + 1.0)
    damping = (
        (moment_count - m + 1.0) * np.cos(step * m) + np.sin(step * m) / math.tan(step)
    ) / (moment_count + 1.0)
    weights = np.where(m == 0, damping, 2.0 * damping)
    angles = math.pi * (np.arange(energy_count // 2) + 0.5) / energy_count
    table = (weights[None, :] * np.cos(angles[:, None] * m[None, :])).astype(np.float32)
    halves = []
    for parity in range(2):
        part = table[:, parity::2]
        high = part.astype(BF16)
        low = (part - high.astype(np.float32)).astype(BF16)
        halves.append(np.concatenate([high, low, high, low], axis=1))
    return halves


def vmem():
    return pl.BlockSpec(memory_space=pltpu.VMEM)


def smem():
    return pl.BlockSpec(memory_space=pltpu.SMEM)


def params(limit=VMEM_LIMIT):
    return pltpu.CompilerParams(vmem_limit_bytes=limit)


def cost(flops, size):
    return pl.CostEstimate(flops=int(flops), bytes_accessed=int(size), transcendentals=0)


def gather_rows(onehot, value):
    high, low = split(value)
    return dot(onehot, jnp.concatenate([high, low], axis=0))


def any_space():
    return pl.BlockSpec(memory_space=pl.ANY)


def hbm():
    return pl.BlockSpec(memory_space=pltpu.HBM)


def stay(x):
    return pltpu.with_memory_space_constraint(x, pltpu.HBM)


def emit_sends(pick, value, columns, send_a, send_b):
    rim = send_a.shape[0]
    got = gather_rows(pick, value)
    send_a[:, columns] = got[:rim]
    send_b[:, columns] = got[rim:]


def first_kernel(rim, index_ref, lists_hbm, cur_hbm, pick_ref, cur_ref, send_a, send_b, lists_ref, sems):
    count, blocks, width = cur_ref.shape
    list_copy = pltpu.make_async_copy(lists_hbm, lists_ref, sems.at[count])
    list_copy.start()
    copies = [pltpu.make_async_copy(cur_hbm.at[v], cur_ref.at[v], sems.at[v]) for v in range(count)]
    for copy in copies:
        copy.start()
    list_copy.wait()
    lists = lists_ref[0]
    even = index_ref[0] == 0
    rows = lax.broadcasted_iota(jnp.int32, (rim, rim), 0)
    lanes = lax.broadcasted_iota(jnp.int32, (rim, rim), 1)
    slots = lax.broadcasted_iota(jnp.int32, (rim, blocks), 1)
    for half in range(2):
        mine = lists[half : half + 1]
        other = lists[1 - half : 2 - half]
        chosen = jnp.where(even, mine, other)
        spread = jnp.where(rows == lanes, chosen, 0).astype(F32)
        column = jnp.sum(spread, axis=1, keepdims=True).astype(jnp.int32)
        onehot = jnp.where(slots == column, 1.0, 0.0).astype(BF16)
        pick_ref[pl.ds(half * rim, rim), 0:blocks] = onehot
        pick_ref[pl.ds(half * rim, rim), blocks : 2 * blocks] = onehot
    pick = pick_ref[...]
    for v in range(count):
        copies[v].wait()
        emit_sends(pick, cur_ref[v], slice(v * width, (v + 1) * width), send_a, send_b)


def prep_kernel(
    rim,
    index_ref,
    cols_hbm,
    ids_hbm,
    pick_ref,
    kinds_hbm,
    cur_hbm,
    prev_hbm,
    probe_hbm,
    site_hbm,
    mix_ref,
    high_ref,
    low_ref,
    prev_ref,
    probe_ref,
    site_ref,
    cur_ref,
    send_a,
    send_b,
    cols_ref,
    ids_ref,
    kinds,
    sems,
):
    links, blocks = cols_ref.shape
    kind_count, width = kinds.shape[:2]
    padded = mix_ref.shape[1] // 2
    copies = [
        pltpu.make_async_copy(kinds_hbm.at[n], kinds.at[n], sems.at[n]) for n in range(kind_count)
    ]
    fetched = ((prev_hbm, prev_ref), (probe_hbm, probe_ref), (site_hbm, site_ref))
    small = [
        pltpu.make_async_copy(cols_hbm, cols_ref, sems.at[kind_count + 3]),
        pltpu.make_async_copy(ids_hbm, ids_ref, sems.at[kind_count + 4]),
    ]
    vecs = cur_ref.shape[0]
    first = cur_hbm.shape[0] - vecs
    for v in range(vecs):
        small.append(
            pltpu.make_async_copy(
                cur_hbm.at[first + v], cur_ref.at[v], sems.at[kind_count + 5 + v]
            )
        )
    for copy in small:
        copy.start()
    for i, (source, target) in enumerate(fetched):
        copies.append(pltpu.make_async_copy(source, target, sems.at[kind_count + i]))
    for copy in copies:
        copy.start()
    even = index_ref[0] == 0
    rows = lax.broadcasted_iota(jnp.int32, (padded, blocks), 0)
    corner = lax.broadcasted_iota(jnp.int32, (blocks, blocks), 0)
    diagonal = corner == lax.broadcasted_iota(jnp.int32, (blocks, blocks), 1)
    identity = jnp.where(diagonal, 1.0, 0.0).astype(BF16)
    for copy in small:
        copy.wait()
    e = cols_ref[...]
    crossed = jnp.where(e < blocks + rim, e + rim, e - rim)
    e = jnp.where(jnp.logical_and(even, e >= blocks), crossed, e)
    ids = ids_ref[...]
    for n in range(kind_count):
        mine = jnp.where(ids == n, e, -1)
        total = jnp.zeros((padded, blocks), F32)
        for k in range(links):
            total += jnp.where(rows == mine[k : k + 1], 1.0, 0.0)
        turned = lax.dot_general(
            identity, total.astype(BF16), (((1,), (1,)), ((), ())), preferred_element_type=F32
        ).astype(BF16)
        mix_ref[n * blocks : (n + 1) * blocks, 0:padded] = turned
        mix_ref[n * blocks : (n + 1) * blocks, padded : 2 * padded] = turned
    for v in range(vecs):
        emit_sends(pick_ref[...], cur_ref[v], slice(v * width, (v + 1) * width), send_a, send_b)
    for n in range(kind_count):
        copies[n].wait()
        high, low = split(2.0 * kinds[n])
        high_ref[n * width : (n + 1) * width] = high
        low_ref[n * width : (n + 1) * width] = low
    for copy in copies[kind_count:]:
        copy.wait()


def step_kernel(
    cfg,
    index_ref,
    mix_ref,
    high_ref,
    low_ref,
    pick_ref,
    site_ref,
    cur_ref,
    prev_ref,
    probe_ref,
    recv_a,
    recv_b,
    *rest,
):
    vecs, cur_at, prev_at, own_at, last, add_partial, older, fold, fetch, aliased = cfg
    rest = list(rest)
    partial_in = rest.pop(0) if add_partial else None
    olders = [rest.pop(0) for _ in range(older)]
    prior_hbm = rest.pop(0) if fetch is not None else None
    rest = rest[aliased:]
    out_ref, partial_out = rest[:2]
    rest = rest[2:]
    if last:
        prev_out = rest.pop(0)
    else:
        send_a, send_b = rest.pop(0), rest.pop(0)
    if fold and last:
        pieces_out = [rest.pop(0) for _ in range(4)]
    elif fold:
        keep_ref, give_ref = rest.pop(0), rest.pop(0)
    if fetch is not None:
        prior_ref = rest.pop(0)
    source, mixed = rest[:2]
    blocks, width = cur_ref.shape[1:]
    rim = recv_a.shape[0]
    padded = source.shape[1] // 2
    kind_count = mix_ref.shape[0] // blocks
    spin = width // 2
    copies = []
    if last:
        copies = [
            pltpu.make_async_copy(
                cur_ref.at[pl.ds(cur_at, vecs)], prev_out.at[pl.ds(own_at, vecs)], rest[2]
            )
        ]
    if fetch is not None:
        halves, _, moments, group, lanes = prior_ref.shape
        known = prior_hbm.shape[0]
        copies = [
            pltpu.make_async_copy(
                prior_hbm.at[:, p, pl.ds(fetch * group, group), pl.ds(h * lanes, lanes)],
                prior_ref.at[h, p, pl.ds(0, known)],
                rest[2].at[2 * h + p],
            )
            for h in range(halves)
            for p in range(2)
        ]
    for copy in copies:
        copy.start()
    if fetch is not None:
        prior_ref[:, :, known:] = jnp.zeros((halves, 2, moments - known, group, lanes), F32)
    for v in range(vecs):
        columns = slice(v * width, (v + 1) * width)
        pieces = [cur_ref[cur_at + v], recv_a[:, columns], recv_b[:, columns]]
        used = blocks + 2 * rim
        if used < padded:
            pieces.append(jnp.zeros((padded - used, width), F32))
        high, low = split(jnp.concatenate(pieces, axis=0))
        source[v, 0:padded] = high
        source[v, padded : 2 * padded] = low
    for v in range(vecs):
        mixture = dot(mix_ref[...], source[v])
        high, low = split(mixture)
        for n in range(kind_count):
            columns = slice(n * width, (n + 1) * width)
            rows = slice(n * blocks, (n + 1) * blocks)
            mixed[v * blocks : (v + 1) * blocks, columns] = high[rows]
            mixed[(vecs + v) * blocks : (vecs + v + 1) * blocks, columns] = low[rows]
    count = vecs * blocks
    both = dot(mixed[...], high_ref[...])
    hopping = both[:count] + both[count:] + dot(mixed[:count], low_ref[...])
    diag_up = 2.0 * (site_ref[0] + site_ref[1])
    diag_down = 2.0 * (site_ref[0] - site_ref[1])
    cross = 2.0 * site_ref[2]
    partial = partial_in[...] if add_partial else None
    for v in range(vecs):
        here = cur_ref[cur_at + v]
        up = here[:, :spin]
        down = here[:, spin:]
        onsite = jnp.concatenate(
            [diag_up * up + cross * down, diag_down * down + cross * up], axis=1
        )
        following = hopping[v * blocks : (v + 1) * blocks] + onsite - prev_ref[prev_at + v]
        out_ref[v] = following
        term = probe_ref[own_at + v] * following
        partial = term if partial is None else partial + term
        if not last:
            columns = slice(v * width, (v + 1) * width)
            emit_sends(pick_ref[...], following, columns, send_a, send_b)
    partial_out[...] = partial
    if fold and last:
        quarter = pieces_out[0].shape[0]
        for flip, piece in enumerate(pieces_out):
            core = index_ref[1] if flip % 2 == 0 else 1 - index_ref[1]
            chip = index_ref[2] if flip < 2 else 1 - index_ref[2]
            at = pl.multiple_of((2 * chip + core) * quarter, quarter)
            piece[...] = partial_out[pl.ds(at, quarter)]
    elif fold:
        cores = 2
        quarter = keep_ref.shape[2]
        core = index_ref[1]
        for s in range(older + 1):
            ref = olders[s] if s < older else partial_out
            for y in range(keep_ref.shape[1]):
                base = y * cores * quarter
                keep_ref[s, y] = ref[pl.ds(pl.multiple_of(base + core * quarter, quarter), quarter)]
                give_ref[s, y] = ref[
                    pl.ds(pl.multiple_of(base + (1 - core) * quarter, quarter), quarter)
                ]
    for copy in copies:
        copy.wait()


def fold_kernel(index_ref, keep_ref, got_ref, mine_ref, give_ref):
    y = index_ref[2]
    mine_ref[...] = keep_ref[:, y] + got_ref[:, y]
    give_ref[...] = keep_ref[:, 1 - y] + got_ref[:, 1 - y]


def energy_kernel(vector_total, chunks, count, even_ref, odd_ref, early_mine, early_got, *rest):
    priors, rest = rest[:count], rest[count:]
    lates, finals = rest[:4], rest[4 : 4 + chunks]
    new_ref, map_out, cur_out, fresh, held, sems = rest[4 + chunks :]
    halves, _, pairs, group, lanes = priors[0].shape
    vecs = finals[0].shape[0]
    copies = [
        pltpu.make_async_copy(
            finals[c], cur_out.at[pl.ds(c * vecs, vecs)], sems.at[count * halves + c]
        )
        for c in range(chunks)
    ]
    for copy in copies:
        copy.start()
    early = early_mine.shape[0]
    steps = new_ref.shape[0]
    scale = 1.0 / vector_total
    new_ref[0:early] = (early_mine[...] + early_got[...]) * scale
    new_ref[early] = ((lates[0][...] + lates[1][...]) + (lates[2][...] + lates[3][...])) * scale
    half = even_ref.shape[0]
    flip = 7 - lax.broadcasted_iota(jnp.int32, (8, lanes), 0)
    for i in range(count):
        for h in range(halves):
            slot = i * halves + h
            rows = slice(i * group, (i + 1) * group)
            columns = slice(h * lanes, (h + 1) * lanes)
            for p in range(2):
                fresh[slot, p, 0 : 8 - steps // 2] = jnp.zeros((8 - steps // 2, group, lanes), F32)
                for m in range(p, steps, 2):
                    fresh[slot, p, 8 - steps // 2 + m // 2] = new_ref[m, rows, columns]
            flat = held.at[slot].reshape(2 * half * group, lanes)
            for b in range(0, group, 2):
                sums = []
                for parity, table in ((0, even_ref), (1, odd_ref)):
                    pair = []
                    for j in range(2):
                        old = priors[i].at[h, parity].reshape(pairs * group, lanes)
                        value = old[pl.ds(b + j, pairs, stride=group)]
                        extra = fresh.at[slot, parity].reshape(8 * group, lanes)
                        added = extra[pl.ds(b + j, 8, stride=group)]
                        pair.append(
                            jnp.concatenate([value[: pairs - 8], value[pairs - 8 :] + added], axis=0)
                        )
                    high, low = split(jnp.concatenate(pair, axis=1))
                    sums.append(dot(table[...], jnp.concatenate([high, high, low, low], axis=0)))
                plus = sums[0] + sums[1]
                minus = sums[0] - sums[1]
                for j in range(2):
                    side = slice(j * lanes, (j + 1) * lanes)
                    flat[pl.ds(b + j, half, stride=group)] = plus[:, side]
                    for r in range(0, half, 8):
                        turned = jnp.take_along_axis(minus[r : r + 8, side], flip, axis=0)
                        top = 2 * half - 8 - r
                        flat[pl.ds(top * group + b + j, 8, stride=group)] = turned
            copy = pltpu.make_async_copy(
                held.at[slot],
                map_out.at[:, pl.ds(i * group, group), pl.ds(h * lanes, lanes)],
                sems.at[slot],
            )
            copy.start()
            copies.append(copy)
    for copy in copies:
        copy.wait()


def per_device(
    probe,
    cheb_prev,
    cheb_cur,
    prior_moments,
    site_terms,
    hop_kinds,
    tile_kind_ids,
    send_lists,
    tile_cols,
):
    group, lanes = 8, 128
    moment_count = prior_moments.shape[0] + STEPS
    vec_dev, blocks, width = cheb_cur.shape
    kind_count = hop_kinds.shape[0]
    groups = lax.axis_size("vec")
    domains = lax.axis_size("dom")
    rim = send_lists.shape[2]
    chunks = 2
    vecs = vec_dev // chunks
    quarter = blocks // groups
    padded = -(-(blocks + 2 * rim) // 256) * 256
    swap_a = [(i, i ^ 1) for i in range(domains)]
    swap_b = [(i, (i + 1) % domains if i % 2 else (i - 1) % domains) for i in range(domains)]
    vec_index = lax.axis_index("vec")
    index = jnp.stack([lax.axis_index("dom") % 2, vec_index % 2, vec_index // 2]).astype(jnp.int32)

    rows = jax.ShapeDtypeStruct((rim, vecs * width), F32)
    full_shape = jax.ShapeDtypeStruct((vec_dev, blocks, width), F32)
    chunk_shape = jax.ShapeDtypeStruct((vecs, blocks, width), F32)
    pick, cur_first, *sends = pl.pallas_call(
        functools.partial(first_kernel, rim),
        out_shape=[jax.ShapeDtypeStruct((2 * rim, 2 * blocks), BF16), chunk_shape, rows, rows],
        in_specs=[smem(), hbm(), hbm()],
        out_specs=[vmem()] * 4,
        scratch_shapes=[
            pltpu.VMEM(send_lists.shape, jnp.int32),
            pltpu.SemaphoreType.DMA((vecs + 1,)),
        ],
        compiler_params=params(),
        cost_estimate=cost(1e8, 1e6),
        name="first_sends",
    )(index, stay(send_lists), stay(cheb_cur))

    def exchange(a, b):
        got_a = lax.ppermute(a, "dom", swap_a)
        got_b = lax.ppermute(b, "dom", swap_b)
        return got_a, got_b

    received = [exchange(*sends)]
    links = tile_cols.shape[1]
    mix, high, low, prev_held, probe_held, site_held, cur_second, *sends = pl.pallas_call(
        functools.partial(prep_kernel, rim),
        out_shape=[
            jax.ShapeDtypeStruct((kind_count * blocks, 2 * padded), BF16),
            jax.ShapeDtypeStruct((kind_count * width, width), BF16),
            jax.ShapeDtypeStruct((kind_count * width, width), BF16),
            full_shape,
            full_shape,
            jax.ShapeDtypeStruct(site_terms.shape, F32),
            chunk_shape,
            rows,
            rows,
        ],
        in_specs=[smem(), hbm(), hbm(), vmem()] + [hbm()] * 5,
        out_specs=[vmem()] * 9,
        scratch_shapes=[
            pltpu.VMEM((links, blocks), jnp.int32),
            pltpu.VMEM((links, blocks), jnp.int32),
            pltpu.VMEM(hop_kinds.shape, F32),
            pltpu.SemaphoreType.DMA((kind_count + 5 + vecs,)),
        ],
        compiler_params=params(),
        cost_estimate=cost(1e7, 8e6),
        name="tables",
    )(
        index,
        stay(tile_cols.T),
        stay(tile_kind_ids.T),
        pick,
        *[stay(x) for x in (hop_kinds, cheb_cur, cheb_prev, probe, site_terms)],
    )
    received.append(exchange(*sends))

    partial_shape = jax.ShapeDtypeStruct((blocks, width), F32)
    current = [(cur_first, 0), (cur_second, 0)]
    previous = [(prev_held, c * vecs) for c in range(chunks)]

    def reduce(keep, give):
        got = lax.ppermute(give, "vec", [(i, i ^ 1) for i in range(groups)])
        piece = jax.ShapeDtypeStruct((keep.shape[0], quarter, width), F32)
        mine, give = pl.pallas_call(
            fold_kernel,
            out_shape=[piece, piece],
            in_specs=[smem(), vmem(), vmem()],
            out_specs=[vmem(), vmem()],
            compiler_params=params(),
            cost_estimate=cost(1e5, 1e6),
            name="fold",
        )(index, keep, got)
        return mine, lax.ppermute(give, "vec", [(i, i ^ 2) for i in range(groups)])

    partials = []
    buffers = []
    prior_held = []
    prior_pairs = prior_moments.reshape(prior_moments.shape[0] // 2, 2, quarter, width)
    for s in range(STEPS):
        last = s == STEPS - 1
        partial = None
        for c in range(chunks):
            args = [index, mix, high, low, pick, site_held]
            args += [current[c][0], previous[c][0], probe_held, *received[c]]
            specs = [smem()] + [vmem()] * (len(args) - 1)
            fold = c == chunks - 1 and s >= STEPS - 2
            older = 0 if last or not fold else len(partials)
            extra = ([] if partial is None else [partial]) + partials[:older]
            args += extra
            specs += [vmem()] * len(extra)
            place = s * chunks + c
            fetch = place if place < quarter // group else None
            if fetch is not None:
                args.append(stay(prior_pairs))
                specs.append(hbm())
            aliases = {len(args) + i: 2 + i for i in range(len(buffers))}
            args += buffers
            specs += [any_space()] * len(buffers)
            scratch = [
                pltpu.VMEM((vecs, 2 * padded, width), BF16),
                pltpu.VMEM((2 * vecs * blocks, kind_count * width), BF16),
            ]
            outs, out_specs = [chunk_shape, partial_shape], [vmem(), vmem()]
            if last:
                outs.append(full_shape)
                out_specs.append(any_space())
                scratch.append(pltpu.SemaphoreType.DMA)
            else:
                outs += [rows, rows]
            if fold and last:
                outs += [jax.ShapeDtypeStruct((quarter, width), F32)] * 4
            elif fold:
                outs += [jax.ShapeDtypeStruct((older + 1, groups // 2, quarter, width), F32)] * 2
            if fetch is not None:
                outs.append(
                    jax.ShapeDtypeStruct((width // lanes, 2, moment_count // 2, group, lanes), F32)
                )
                scratch.append(pltpu.SemaphoreType.DMA((2 * (width // lanes),)))
            out_specs += [vmem()] * (len(outs) - len(out_specs))
            cfg = (
                vecs,
                current[c][1],
                previous[c][1],
                c * vecs,
                last,
                partial is not None,
                older,
                fold,
                fetch,
                len(buffers),
            )
            result = list(
                pl.pallas_call(
                    functools.partial(step_kernel, cfg),
                    out_shape=outs,
                    in_specs=specs,
                    out_specs=out_specs,
                    scratch_shapes=scratch,
                    input_output_aliases=aliases,
                    compiler_params=pltpu.CompilerParams(vmem_limit_bytes=VMEM_LIMIT),
                    cost_estimate=cost(1.5e9, 5e6),
                )(*args)
            )
            previous[c], current[c] = current[c], (result.pop(0), 0)
            partial = result.pop(0)
            if last:
                buffers = [result.pop(0)]
            else:
                received[c] = exchange(result.pop(0), result.pop(0))
            if fetch is not None:
                prior_held.append(result.pop(0))
            if fold and last:
                lates = [result[0]]
                for flip in (2, 3, 1):
                    pairs = [(i, i ^ flip) for i in range(groups)]
                    lates.append(lax.ppermute(result[flip], "vec", pairs))
            elif fold:
                early = reduce(*result)
        partials.append(partial)

    tables = [jnp.asarray(x) for x in jackson_split(moment_count, ENERGIES)]
    tiles = quarter // group * (width // lanes)
    args = [*tables, *early, *prior_held, *lates, *[current[c][0] for c in range(chunks)]]
    new_moments, energy_map, next_cur = pl.pallas_call(
        functools.partial(energy_kernel, vec_dev * groups, chunks, len(prior_held)),
        out_shape=[
            jax.ShapeDtypeStruct((STEPS, quarter, width), F32),
            jax.ShapeDtypeStruct((ENERGIES, quarter, width), F32),
            full_shape,
        ],
        in_specs=[vmem()] * len(args),
        out_specs=[vmem(), any_space(), any_space()],
        scratch_shapes=[
            pltpu.VMEM((tiles, 2, 8, group, lanes), F32),
            pltpu.VMEM((tiles, ENERGIES, group, lanes), F32),
            pltpu.SemaphoreType.DMA((tiles + chunks,)),
        ],
        compiler_params=params(),
        cost_estimate=cost(4e9, 2.2e7),
        name="energy",
    )(*args)
    return buffers[0], next_cur, new_moments, energy_map


def solution(mesh):
    return jax.shard_map(
        per_device,
        mesh=mesh,
        in_specs=(
            P("vec", "dom", None),
            P("vec", "dom", None),
            P("vec", "dom", None),
            P(None, ("dom", "vec"), None),
            P(None, "dom", None),
            P(),
            P("dom", None),
            P("dom", None, None),
            P("dom", None),
        ),
        out_specs=(
            P("vec", "dom", None),
            P("vec", "dom", None),
            P(None, ("dom", "vec"), None),
            P(None, ("dom", "vec"), None),
        ),
        check_vma=False,
    )
```

```python
import functools
import math

import jax
import jax.numpy as jnp
import numpy as np
from jax import lax
from jax.experimental import pallas as pl
from jax.experimental.pallas import tpu as pltpu
from jax.sharding import PartitionSpec as P


ENERGIES = 512
STEPS = 4
F32 = jnp.float32
BF16 = jnp.bfloat16
VMEM_LIMIT = 24 * 1024 * 1024


def split(x):
    high = x.astype(BF16)
    return high, (x - high.astype(F32)).astype(BF16)


def dot(a, b):
    return jnp.dot(a, b, preferred_element_type=F32)


def jackson_split(moment_count, energy_count):
    m = np.arange(moment_count, dtype=np.float64)
    step = math.pi / (moment_count + 1.0)
    damping = (
        (moment_count - m + 1.0) * np.cos(step * m) + np.sin(step * m) / math.tan(step)
    ) / (moment_count + 1.0)
    weights = np.where(m == 0, damping, 2.0 * damping)
    angles = math.pi * (np.arange(energy_count // 2) + 0.5) / energy_count
    table = (weights[None, :] * np.cos(angles[:, None] * m[None, :])).astype(np.float32)
    halves = []
    for parity in range(2):
        part = table[:, parity::2]
        high = part.astype(BF16)
        low = (part - high.astype(np.float32)).astype(BF16)
        halves.append(np.concatenate([high, low, high, low], axis=1))
    return halves


def vmem():
    return pl.BlockSpec(memory_space=pltpu.VMEM)


def params(limit=VMEM_LIMIT):
    return pltpu.CompilerParams(vmem_limit_bytes=limit)


def cost(flops, size):
    return pl.CostEstimate(flops=int(flops), bytes_accessed=int(size), transcendentals=0)


def choose(index_ref, which, when_zero, when_one):
    rows, width = when_zero.shape
    bit = jnp.broadcast_to(index_ref[which, 0:1, 0:1], (rows, width))
    return jnp.where(bit == 0, when_zero, when_one)


def gather_rows(onehot, value):
    high, low = split(value)
    return dot(onehot, jnp.concatenate([high, low], axis=0))


def any_space():
    return pl.BlockSpec(memory_space=pl.ANY)


def hbm():
    return pl.BlockSpec(memory_space=pltpu.HBM)


def stay(x):
    return pltpu.with_memory_space_constraint(x, pltpu.HBM)


def emit_sends(pick, value, columns, send_a, send_b):
    rim = send_a.shape[0]
    got = gather_rows(pick, value)
    send_a[:, columns] = got[:rim]
    send_b[:, columns] = got[rim:]


def first_kernel(rim, index_ref, lists_hbm, cur_hbm, pick_ref, cur_ref, send_a, send_b, lists_ref, sems):
    count, blocks, width = cur_ref.shape
    list_copy = pltpu.make_async_copy(lists_hbm, lists_ref, sems.at[count])
    list_copy.start()
    copies = [pltpu.make_async_copy(cur_hbm.at[v], cur_ref.at[v], sems.at[v]) for v in range(count)]
    for copy in copies:
        copy.start()
    list_copy.wait()
    lists = lists_ref[0]
    rows = lax.broadcasted_iota(jnp.int32, (rim, rim), 0)
    lanes = lax.broadcasted_iota(jnp.int32, (rim, rim), 1)
    slots = lax.broadcasted_iota(jnp.int32, (rim, blocks), 1)
    for half in range(2):
        mine = lists[half : half + 1]
        other = lists[1 - half : 2 - half]
        chosen = choose(index_ref, 0, mine, other)
        spread = jnp.where(rows == lanes, chosen, 0).astype(F32)
        column = jnp.sum(spread, axis=1, keepdims=True).astype(jnp.int32)
        onehot = jnp.where(slots == column, 1.0, 0.0).astype(BF16)
        pick_ref[pl.ds(half * rim, rim), 0:blocks] = onehot
        pick_ref[pl.ds(half * rim, rim), blocks : 2 * blocks] = onehot
    pick = pick_ref[...]
    for v in range(count):
        copies[v].wait()
        emit_sends(pick, cur_ref[v], slice(v * width, (v + 1) * width), send_a, send_b)


def prep_kernel(
    rim,
    index_ref,
    cols_hbm,
    ids_hbm,
    pick_ref,
    kinds_hbm,
    cur_hbm,
    prev_hbm,
    probe_hbm,
    site_hbm,
    mix_ref,
    high_ref,
    low_ref,
    prev_ref,
    probe_ref,
    site_ref,
    cur_ref,
    send_a,
    send_b,
    cols_ref,
    ids_ref,
    kinds,
    sems,
):
    links, blocks = cols_ref.shape
    kind_count, width = kinds.shape[:2]
    padded = mix_ref.shape[1] // 2
    copies = [
        pltpu.make_async_copy(kinds_hbm.at[n], kinds.at[n], sems.at[n]) for n in range(kind_count)
    ]
    fetched = ((prev_hbm, prev_ref), (probe_hbm, probe_ref), (site_hbm, site_ref))
    small = [
        pltpu.make_async_copy(cols_hbm, cols_ref, sems.at[kind_count + 3]),
        pltpu.make_async_copy(ids_hbm, ids_ref, sems.at[kind_count + 4]),
    ]
    vecs = cur_ref.shape[0]
    first = cur_hbm.shape[0] - vecs
    for v in range(vecs):
        small.append(
            pltpu.make_async_copy(
                cur_hbm.at[first + v], cur_ref.at[v], sems.at[kind_count + 5 + v]
            )
        )
    for copy in small:
        copy.start()
    for i, (source, target) in enumerate(fetched):
        copies.append(pltpu.make_async_copy(source, target, sems.at[kind_count + i]))
    for copy in copies:
        copy.start()
    rows = lax.broadcasted_iota(jnp.int32, (padded, blocks), 0)
    corner = lax.broadcasted_iota(jnp.int32, (blocks, blocks), 0)
    diagonal = corner == lax.broadcasted_iota(jnp.int32, (blocks, blocks), 1)
    identity = jnp.where(diagonal, 1.0, 0.0).astype(BF16)
    for copy in small:
        copy.wait()
    e = cols_ref[...]
    crossed = jnp.where(e < blocks + rim, e + rim, e - rim)
    e = choose(index_ref, 0, jnp.where(e >= blocks, crossed, e), e)
    ids = ids_ref[...]
    for n in range(kind_count):
        mine = jnp.where(ids == n, e, -1)
        total = jnp.zeros((padded, blocks), F32)
        for k in range(links):
            total += jnp.where(rows == mine[k : k + 1], 1.0, 0.0)
        turned = lax.dot_general(
            identity, total.astype(BF16), (((1,), (1,)), ((), ())), preferred_element_type=F32
        ).astype(BF16)
        mix_ref[n * blocks : (n + 1) * blocks, 0:padded] = turned
        mix_ref[n * blocks : (n + 1) * blocks, padded : 2 * padded] = turned
    for v in range(vecs):
        emit_sends(pick_ref[...], cur_ref[v], slice(v * width, (v + 1) * width), send_a, send_b)
    for n in range(kind_count):
        copies[n].wait()
        high, low = split(2.0 * kinds[n])
        high_ref[n * width : (n + 1) * width] = high
        low_ref[n * width : (n + 1) * width] = low
    for copy in copies[kind_count:]:
        copy.wait()


def step_kernel(
    cfg,
    index_ref,
    mix_ref,
    high_ref,
    low_ref,
    pick_ref,
    site_ref,
    cur_ref,
    prev_ref,
    probe_ref,
    recv_a,
    recv_b,
    *rest,
):
    vecs, cur_at, prev_at, own_at, last, add_partial, older, fold, fetch, aliased = cfg
    rest = list(rest)
    partial_in = rest.pop(0) if add_partial else None
    olders = [rest.pop(0) for _ in range(older)]
    prior_hbm = rest.pop(0) if fetch is not None else None
    rest = rest[aliased:]
    out_ref, partial_out = rest[:2]
    rest = rest[2:]
    if last:
        prev_out = rest.pop(0)
    else:
        send_a, send_b = rest.pop(0), rest.pop(0)
    if fold and last:
        pieces_out = [rest.pop(0) for _ in range(4)]
    elif fold:
        keep_ref, give_ref = rest.pop(0), rest.pop(0)
    if fetch is not None:
        prior_ref = rest.pop(0)
    source, mixed = rest[:2]
    blocks, width = cur_ref.shape[1:]
    rim = recv_a.shape[0]
    padded = source.shape[1] // 2
    kind_count = mix_ref.shape[0] // blocks
    spin = width // 2
    copies = []
    if last:
        copies = [
            pltpu.make_async_copy(
                cur_ref.at[pl.ds(cur_at, vecs)], prev_out.at[pl.ds(own_at, vecs)], rest[2]
            )
        ]
    if fetch is not None:
        halves, _, moments, group, lanes = prior_ref.shape
        known = prior_hbm.shape[0]
        copies = [
            pltpu.make_async_copy(
                prior_hbm.at[:, p, pl.ds(fetch * group, group), pl.ds(h * lanes, lanes)],
                prior_ref.at[h, p, pl.ds(0, known)],
                rest[2].at[2 * h + p],
            )
            for h in range(halves)
            for p in range(2)
        ]
    for copy in copies:
        copy.start()
    if fetch is not None:
        prior_ref[:, :, known:] = jnp.zeros((halves, 2, moments - known, group, lanes), F32)
    for v in range(vecs):
        columns = slice(v * width, (v + 1) * width)
        pieces = [cur_ref[cur_at + v], recv_a[:, columns], recv_b[:, columns]]
        used = blocks + 2 * rim
        if used < padded:
            pieces.append(jnp.zeros((padded - used, width), F32))
        high, low = split(jnp.concatenate(pieces, axis=0))
        source[v, 0:padded] = high
        source[v, padded : 2 * padded] = low
    for v in range(vecs):
        mixture = dot(mix_ref[...], source[v])
        high, low = split(mixture)
        for n in range(kind_count):
            columns = slice(n * width, (n + 1) * width)
            rows = slice(n * blocks, (n + 1) * blocks)
            mixed[v * blocks : (v + 1) * blocks, columns] = high[rows]
            mixed[(vecs + v) * blocks : (vecs + v + 1) * blocks, columns] = low[rows]
    count = vecs * blocks
    both = dot(mixed[...], high_ref[...])
    hopping = both[:count] + both[count:] + dot(mixed[:count], low_ref[...])
    diag_up = 2.0 * (site_ref[0] + site_ref[1])
    diag_down = 2.0 * (site_ref[0] - site_ref[1])
    cross = 2.0 * site_ref[2]
    partial = partial_in[...] if add_partial else None
    for v in range(vecs):
        here = cur_ref[cur_at + v]
        up = here[:, :spin]
        down = here[:, spin:]
        onsite = jnp.concatenate(
            [diag_up * up + cross * down, diag_down * down + cross * up], axis=1
        )
        following = hopping[v * blocks : (v + 1) * blocks] + onsite - prev_ref[prev_at + v]
        out_ref[v] = following
        term = probe_ref[own_at + v] * following
        partial = term if partial is None else partial + term
        if not last:
            columns = slice(v * width, (v + 1) * width)
            emit_sends(pick_ref[...], following, columns, send_a, send_b)
    partial_out[...] = partial
    if fold:
        quarter = blocks // 4
        for s in range(older + 1):
            ref = olders[s] if s < older else partial_out
            parts = [ref[i * quarter : (i + 1) * quarter] for i in range(4)]
            keep = [choose(index_ref, 1, *parts[2 * y : 2 * y + 2]) for y in range(2)]
            give = [choose(index_ref, 1, *parts[2 * y : 2 * y + 2][::-1]) for y in range(2)]
            if last:
                pieces_out[0][...] = choose(index_ref, 2, *keep)
                pieces_out[1][...] = choose(index_ref, 2, *give)
                pieces_out[2][...] = choose(index_ref, 2, *keep[::-1])
                pieces_out[3][...] = choose(index_ref, 2, *give[::-1])
            else:
                for y in range(2):
                    keep_ref[s, y] = keep[y]
                    give_ref[s, y] = give[y]
    for copy in copies:
        copy.wait()


def fold_kernel(index_ref, keep_ref, got_ref, mine_ref, give_ref):
    for s in range(keep_ref.shape[0]):
        sums = [keep_ref[s, y] + got_ref[s, y] for y in range(2)]
        mine_ref[s] = choose(index_ref, 2, *sums)
        give_ref[s] = choose(index_ref, 2, *sums[::-1])


def energy_kernel(vector_total, chunks, count, even_ref, odd_ref, early_mine, early_got, *rest):
    priors, rest = rest[:count], rest[count:]
    lates, finals = rest[:4], rest[4 : 4 + chunks]
    new_ref, map_out, cur_out, fresh, held, sems = rest[4 + chunks :]
    halves, _, pairs, group, lanes = priors[0].shape
    vecs = finals[0].shape[0]
    copies = [
        pltpu.make_async_copy(
            finals[c], cur_out.at[pl.ds(c * vecs, vecs)], sems.at[count * halves + c]
        )
        for c in range(chunks)
    ]
    for copy in copies:
        copy.start()
    early = early_mine.shape[0]
    steps = new_ref.shape[0]
    scale = 1.0 / vector_total
    new_ref[0:early] = (early_mine[...] + early_got[...]) * scale
    new_ref[early] = ((lates[0][...] + lates[1][...]) + (lates[2][...] + lates[3][...])) * scale
    half = even_ref.shape[0]
    flip = 7 - lax.broadcasted_iota(jnp.int32, (8, lanes), 0)
    for i in range(count):
        for h in range(halves):
            slot = i * halves + h
            rows = slice(i * group, (i + 1) * group)
            columns = slice(h * lanes, (h + 1) * lanes)
            for p in range(2):
                fresh[slot, p, 0 : 8 - steps // 2] = jnp.zeros((8 - steps // 2, group, lanes), F32)
                for m in range(p, steps, 2):
                    fresh[slot, p, 8 - steps // 2 + m // 2] = new_ref[m, rows, columns]
            flat = held.at[slot].reshape(2 * half * group, lanes)
            for b in range(0, group, 2):
                sums = []
                for parity, table in ((0, even_ref), (1, odd_ref)):
                    pair = []
                    for j in range(2):
                        old = priors[i].at[h, parity].reshape(pairs * group, lanes)
                        value = old[pl.ds(b + j, pairs, stride=group)]
                        extra = fresh.at[slot, parity].reshape(8 * group, lanes)
                        added = extra[pl.ds(b + j, 8, stride=group)]
                        pair.append(
                            jnp.concatenate([value[: pairs - 8], value[pairs - 8 :] + added], axis=0)
                        )
                    high, low = split(jnp.concatenate(pair, axis=1))
                    sums.append(dot(table[...], jnp.concatenate([high, high, low, low], axis=0)))
                plus = sums[0] + sums[1]
                minus = sums[0] - sums[1]
                for j in range(2):
                    side = slice(j * lanes, (j + 1) * lanes)
                    flat[pl.ds(b + j, half, stride=group)] = plus[:, side]
                    for r in range(0, half, 8):
                        turned = jnp.take_along_axis(minus[r : r + 8, side], flip, axis=0)
                        top = 2 * half - 8 - r
                        flat[pl.ds(top * group + b + j, 8, stride=group)] = turned
            copy = pltpu.make_async_copy(
                held.at[slot],
                map_out.at[:, pl.ds(i * group, group), pl.ds(h * lanes, lanes)],
                sems.at[slot],
            )
            copy.start()
            copies.append(copy)
    for copy in copies:
        copy.wait()


def per_device(
    probe,
    cheb_prev,
    cheb_cur,
    prior_moments,
    site_terms,
    hop_kinds,
    tile_kind_ids,
    send_lists,
    tile_cols,
):
    group, lanes = 8, 128
    moment_count = prior_moments.shape[0] + STEPS
    vec_dev, blocks, width = cheb_cur.shape
    kind_count = hop_kinds.shape[0]
    groups = lax.axis_size("vec")
    domains = lax.axis_size("dom")
    rim = send_lists.shape[2]
    chunks = 2
    vecs = vec_dev // chunks
    quarter = blocks // groups
    padded = -(-(blocks + 2 * rim) // 256) * 256
    swap_a = [(i, i ^ 1) for i in range(domains)]
    swap_b = [(i, (i + 1) % domains if i % 2 else (i - 1) % domains) for i in range(domains)]
    vec_index = lax.axis_index("vec")
    index = jnp.stack([lax.axis_index("dom") % 2, vec_index % 2, vec_index // 2]).astype(jnp.int32)
    index = jnp.broadcast_to(index[:, None, None], (3, 8, 128))

    rows = jax.ShapeDtypeStruct((rim, vecs * width), F32)
    full_shape = jax.ShapeDtypeStruct((vec_dev, blocks, width), F32)
    chunk_shape = jax.ShapeDtypeStruct((vecs, blocks, width), F32)
    pick, cur_first, *sends = pl.pallas_call(
        functools.partial(first_kernel, rim),
        out_shape=[jax.ShapeDtypeStruct((2 * rim, 2 * blocks), BF16), chunk_shape, rows, rows],
        in_specs=[vmem(), hbm(), hbm()],
        out_specs=[vmem()] * 4,
        scratch_shapes=[
            pltpu.VMEM(send_lists.shape, jnp.int32),
            pltpu.SemaphoreType.DMA((vecs + 1,)),
        ],
        compiler_params=params(),
        cost_estimate=cost(1e8, 1e6),
        name="first_sends",
    )(index, stay(send_lists), stay(cheb_cur))

    def exchange(a, b):
        got_a = lax.ppermute(a, "dom", swap_a)
        got_b = lax.ppermute(b, "dom", swap_b)
        return got_a, got_b

    received = [exchange(*sends)]
    links = tile_cols.shape[1]
    mix, high, low, prev_held, probe_held, site_held, cur_second, *sends = pl.pallas_call(
        functools.partial(prep_kernel, rim),
        out_shape=[
            jax.ShapeDtypeStruct((kind_count * blocks, 2 * padded), BF16),
            jax.ShapeDtypeStruct((kind_count * width, width), BF16),
            jax.ShapeDtypeStruct((kind_count * width, width), BF16),
            full_shape,
            full_shape,
            jax.ShapeDtypeStruct(site_terms.shape, F32),
            chunk_shape,
            rows,
            rows,
        ],
        in_specs=[vmem(), hbm(), hbm(), vmem()] + [hbm()] * 5,
        out_specs=[vmem()] * 9,
        scratch_shapes=[
            pltpu.VMEM((links, blocks), jnp.int32),
            pltpu.VMEM((links, blocks), jnp.int32),
            pltpu.VMEM(hop_kinds.shape, F32),
            pltpu.SemaphoreType.DMA((kind_count + 5 + vecs,)),
        ],
        compiler_params=params(),
        cost_estimate=cost(1e7, 8e6),
        name="tables",
    )(
        index,
        stay(tile_cols.T),
        stay(tile_kind_ids.T),
        pick,
        *[stay(x) for x in (hop_kinds, cheb_cur, cheb_prev, probe, site_terms)],
    )
    received.append(exchange(*sends))

    partial_shape = jax.ShapeDtypeStruct((blocks, width), F32)
    current = [(cur_first, 0), (cur_second, 0)]
    previous = [(prev_held, c * vecs) for c in range(chunks)]

    def reduce(keep, give):
        got = lax.ppermute(give, "vec", [(i, i ^ 1) for i in range(groups)])
        piece = jax.ShapeDtypeStruct((keep.shape[0], quarter, width), F32)
        mine, give = pl.pallas_call(
            fold_kernel,
            out_shape=[piece, piece],
            in_specs=[vmem()] * 3,
            out_specs=[vmem()] * 2,
            compiler_params=params(),
            cost_estimate=cost(1e5, 1e6),
            name="fold",
        )(index, keep, got)
        return mine, lax.ppermute(give, "vec", [(i, i ^ 2) for i in range(groups)])

    partials = []
    buffers = []
    prior_held = []
    prior_pairs = prior_moments.reshape(prior_moments.shape[0] // 2, 2, quarter, width)
    for s in range(STEPS):
        last = s == STEPS - 1
        partial = None
        for c in range(chunks):
            args = [index, mix, high, low, pick, site_held]
            args += [current[c][0], previous[c][0], probe_held, *received[c]]
            specs = [vmem()] * len(args)
            fold = c == chunks - 1 and s >= STEPS - 2
            older = 0 if last or not fold else len(partials)
            extra = ([] if partial is None else [partial]) + partials[:older]
            args += extra
            specs += [vmem()] * len(extra)
            place = s * chunks + c
            fetch = place if place < quarter // group else None
            if fetch is not None:
                args.append(stay(prior_pairs))
                specs.append(hbm())
            aliases = {len(args) + i: 2 + i for i in range(len(buffers))}
            args += buffers
            specs += [any_space()] * len(buffers)
            scratch = [
                pltpu.VMEM((vecs, 2 * padded, width), BF16),
                pltpu.VMEM((2 * vecs * blocks, kind_count * width), BF16),
            ]
            outs, out_specs = [chunk_shape, partial_shape], [vmem(), vmem()]
            if last:
                outs.append(full_shape)
                out_specs.append(any_space())
                scratch.append(pltpu.SemaphoreType.DMA)
            else:
                outs += [rows, rows]
            if fold and last:
                outs += [jax.ShapeDtypeStruct((quarter, width), F32)] * 4
            elif fold:
                outs += [jax.ShapeDtypeStruct((older + 1, groups // 2, quarter, width), F32)] * 2
            if fetch is not None:
                outs.append(
                    jax.ShapeDtypeStruct((width // lanes, 2, moment_count // 2, group, lanes), F32)
                )
                scratch.append(pltpu.SemaphoreType.DMA((2 * (width // lanes),)))
            out_specs += [vmem()] * (len(outs) - len(out_specs))
            cfg = (
                vecs,
                current[c][1],
                previous[c][1],
                c * vecs,
                last,
                partial is not None,
                older,
                fold,
                fetch,
                len(buffers),
            )
            result = list(
                pl.pallas_call(
                    functools.partial(step_kernel, cfg),
                    out_shape=outs,
                    in_specs=specs,
                    out_specs=out_specs,
                    scratch_shapes=scratch,
                    input_output_aliases=aliases,
                    compiler_params=pltpu.CompilerParams(vmem_limit_bytes=VMEM_LIMIT),
                    cost_estimate=cost(1.5e9, 5e6),
                )(*args)
            )
            previous[c], current[c] = current[c], (result.pop(0), 0)
            partial = result.pop(0)
            if last:
                buffers = [result.pop(0)]
            else:
                received[c] = exchange(result.pop(0), result.pop(0))
            if fetch is not None:
                prior_held.append(result.pop(0))
            if fold and last:
                lates = [result[0]]
                for flip in (2, 3, 1):
                    pairs = [(i, i ^ flip) for i in range(groups)]
                    lates.append(lax.ppermute(result[flip], "vec", pairs))
            elif fold:
                early = reduce(*result)
        partials.append(partial)

    tables = [jnp.asarray(x) for x in jackson_split(moment_count, ENERGIES)]
    tiles = quarter // group * (width // lanes)
    args = [*tables, *early, *prior_held, *lates, *[current[c][0] for c in range(chunks)]]
    new_moments, energy_map, next_cur = pl.pallas_call(
        functools.partial(energy_kernel, vec_dev * groups, chunks, len(prior_held)),
        out_shape=[
            jax.ShapeDtypeStruct((STEPS, quarter, width), F32),
            jax.ShapeDtypeStruct((ENERGIES, quarter, width), F32),
            full_shape,
        ],
        in_specs=[vmem()] * len(args),
        out_specs=[vmem(), any_space(), any_space()],
        scratch_shapes=[
            pltpu.VMEM((tiles, 2, 8, group, lanes), F32),
            pltpu.VMEM((tiles, ENERGIES, group, lanes), F32),
            pltpu.SemaphoreType.DMA((tiles + chunks,)),
        ],
        compiler_params=params(),
        cost_estimate=cost(4e9, 2.2e7),
        name="energy",
    )(*args)
    return buffers[0], next_cur, new_moments, energy_map


def solution(mesh):
    return jax.shard_map(
        per_device,
        mesh=mesh,
        in_specs=(
            P("vec", "dom", None),
            P("vec", "dom", None),
            P("vec", "dom", None),
            P(None, ("dom", "vec"), None),
            P(None, "dom", None),
            P(),
            P("dom", None),
            P("dom", None, None),
            P("dom", None),
        ),
        out_specs=(
            P("vec", "dom", None),
            P("vec", "dom", None),
            P(None, ("dom", "vec"), None),
            P(None, ("dom", "vec"), None),
        ),
        check_vma=False,
    )
```

```python
import functools
import math

import jax
import jax.numpy as jnp
import numpy as np
from jax import lax
from jax.experimental import pallas as pl
from jax.experimental.pallas import tpu as pltpu
from jax.sharding import PartitionSpec as P


ENERGIES = 512
STEPS = 4
F32 = jnp.float32
BF16 = jnp.bfloat16
VMEM_LIMIT = 24 * 1024 * 1024


def split(x):
    high = x.astype(BF16)
    return high, (x - high.astype(F32)).astype(BF16)


def dot(a, b):
    return jnp.dot(a, b, preferred_element_type=F32)


def jackson_split(moment_count, energy_count):
    m = np.arange(moment_count, dtype=np.float64)
    step = math.pi / (moment_count + 1.0)
    damping = (
        (moment_count - m + 1.0) * np.cos(step * m) + np.sin(step * m) / math.tan(step)
    ) / (moment_count + 1.0)
    weights = np.where(m == 0, damping, 2.0 * damping)
    angles = math.pi * (np.arange(energy_count // 2) + 0.5) / energy_count
    table = (weights[None, :] * np.cos(angles[:, None] * m[None, :])).astype(np.float32)
    halves = []
    for parity in range(2):
        part = table[:, parity::2]
        high = part.astype(BF16)
        low = (part - high.astype(np.float32)).astype(BF16)
        halves.append(np.concatenate([high, low, high, low], axis=1))
    return halves


def vmem():
    return pl.BlockSpec(memory_space=pltpu.VMEM)


def params(limit=VMEM_LIMIT):
    return pltpu.CompilerParams(vmem_limit_bytes=limit)


def cost(flops, size):
    return pl.CostEstimate(flops=int(flops), bytes_accessed=int(size), transcendentals=0)


def choose(index_ref, which, when_zero, when_one):
    rows, width = when_zero.shape
    bit = jnp.broadcast_to(index_ref[which, 0:1, 0:1], (rows, width))
    return jnp.where(bit == 0, when_zero, when_one)


def gather_rows(onehot, value):
    high, low = split(value)
    return dot(onehot, jnp.concatenate([high, low], axis=0))


def any_space():
    return pl.BlockSpec(memory_space=pl.ANY)


def hbm():
    return pl.BlockSpec(memory_space=pltpu.HBM)


def stay(x):
    return pltpu.with_memory_space_constraint(x, pltpu.HBM)


def emit_sends(pick, value, columns, send_a, send_b):
    rim = send_a.shape[0]
    got = gather_rows(pick, value)
    send_a[:, columns] = got[:rim]
    send_b[:, columns] = got[rim:]


def first_kernel(rim, index_ref, lists_hbm, cur_hbm, pick_ref, cur_ref, send_a, send_b, lists_ref, sems):
    count, blocks, width = cur_ref.shape
    list_copy = pltpu.make_async_copy(lists_hbm, lists_ref, sems.at[count])
    list_copy.start()
    copies = [pltpu.make_async_copy(cur_hbm.at[v], cur_ref.at[v], sems.at[v]) for v in range(count)]
    for copy in copies:
        copy.start()
    list_copy.wait()
    lists = lists_ref[0]
    rows = lax.broadcasted_iota(jnp.int32, (rim, rim), 0)
    lanes = lax.broadcasted_iota(jnp.int32, (rim, rim), 1)
    slots = lax.broadcasted_iota(jnp.int32, (rim, blocks), 1)
    for half in range(2):
        mine = lists[half : half + 1]
        other = lists[1 - half : 2 - half]
        chosen = choose(index_ref, 0, mine, other)
        spread = jnp.where(rows == lanes, chosen, 0).astype(F32)
        column = jnp.sum(spread, axis=1, keepdims=True).astype(jnp.int32)
        onehot = jnp.where(slots == column, 1.0, 0.0).astype(BF16)
        pick_ref[pl.ds(half * rim, rim), 0:blocks] = onehot
        pick_ref[pl.ds(half * rim, rim), blocks : 2 * blocks] = onehot
    pick = pick_ref[...]
    for v in range(count):
        copies[v].wait()
        emit_sends(pick, cur_ref[v], slice(v * width, (v + 1) * width), send_a, send_b)


def prep_kernel(
    rim,
    index_ref,
    cols_hbm,
    ids_hbm,
    pick_ref,
    kinds_hbm,
    cur_hbm,
    prev_hbm,
    probe_hbm,
    site_hbm,
    mix_ref,
    high_ref,
    low_ref,
    prev_ref,
    probe_ref,
    site_ref,
    cur_ref,
    send_a,
    send_b,
    cols_ref,
    ids_ref,
    kinds,
    sems,
):
    links, blocks = cols_ref.shape
    kind_count, width = kinds.shape[:2]
    padded = mix_ref.shape[1] // 2
    copies = [
        pltpu.make_async_copy(kinds_hbm.at[n], kinds.at[n], sems.at[n]) for n in range(kind_count)
    ]
    fetched = ((prev_hbm, prev_ref), (probe_hbm, probe_ref), (site_hbm, site_ref))
    small = [
        pltpu.make_async_copy(cols_hbm, cols_ref, sems.at[kind_count + 3]),
        pltpu.make_async_copy(ids_hbm, ids_ref, sems.at[kind_count + 4]),
    ]
    vecs = cur_ref.shape[0]
    first = cur_hbm.shape[0] - vecs
    for v in range(vecs):
        small.append(
            pltpu.make_async_copy(
                cur_hbm.at[first + v], cur_ref.at[v], sems.at[kind_count + 5 + v]
            )
        )
    for copy in small:
        copy.start()
    for i, (source, target) in enumerate(fetched):
        copies.append(pltpu.make_async_copy(source, target, sems.at[kind_count + i]))
    for copy in copies:
        copy.start()
    rows = lax.broadcasted_iota(jnp.int32, (padded, blocks), 0)
    corner = lax.broadcasted_iota(jnp.int32, (blocks, blocks), 0)
    diagonal = corner == lax.broadcasted_iota(jnp.int32, (blocks, blocks), 1)
    identity = jnp.where(diagonal, 1.0, 0.0).astype(BF16)
    for copy in small:
        copy.wait()
    e = cols_ref[...]
    crossed = jnp.where(e < blocks + rim, e + rim, e - rim)
    e = choose(index_ref, 0, jnp.where(e >= blocks, crossed, e), e)
    ids = ids_ref[...]
    for n in range(kind_count):
        mine = jnp.where(ids == n, e, -1)
        total = jnp.zeros((padded, blocks), F32)
        for k in range(links):
            total += jnp.where(rows == mine[k : k + 1], 1.0, 0.0)
        turned = lax.dot_general(
            identity, total.astype(BF16), (((1,), (1,)), ((), ())), preferred_element_type=F32
        ).astype(BF16)
        mix_ref[n * blocks : (n + 1) * blocks, 0:padded] = turned
        mix_ref[n * blocks : (n + 1) * blocks, padded : 2 * padded] = turned
    for v in range(vecs):
        emit_sends(pick_ref[...], cur_ref[v], slice(v * width, (v + 1) * width), send_a, send_b)
    for n in range(kind_count):
        copies[n].wait()
        high, low = split(2.0 * kinds[n])
        high_ref[n * width : (n + 1) * width] = high
        low_ref[n * width : (n + 1) * width] = low
    for copy in copies[kind_count:]:
        copy.wait()


def step_kernel(
    cfg,
    index_ref,
    mix_ref,
    high_ref,
    low_ref,
    pick_ref,
    site_ref,
    cur_ref,
    prev_ref,
    probe_ref,
    recv_a,
    recv_b,
    *rest,
):
    vecs, cur_at, prev_at, own_at, last, add_partial, older, fold, fetch, aliased = cfg
    rest = list(rest)
    partial_in = rest.pop(0) if add_partial else None
    olders = [rest.pop(0) for _ in range(older)]
    prior_hbm = rest.pop(0) if fetch is not None else None
    rest = rest[aliased:]
    out_ref, partial_out = rest[:2]
    rest = rest[2:]
    if last:
        prev_out = rest.pop(0)
    else:
        send_a, send_b = rest.pop(0), rest.pop(0)
    if fold and not older:
        pieces_out = [rest.pop(0) for _ in range(4)]
    elif fold:
        keep_ref, give_ref = rest.pop(0), rest.pop(0)
    if fetch is not None:
        prior_ref = rest.pop(0)
    source, mixed = rest[:2]
    blocks, width = cur_ref.shape[1:]
    rim = recv_a.shape[0]
    padded = source.shape[1] // 2
    kind_count = mix_ref.shape[0] // blocks
    spin = width // 2
    copies = []
    if last:
        copies = [
            pltpu.make_async_copy(
                cur_ref.at[pl.ds(cur_at, vecs)], prev_out.at[pl.ds(own_at, vecs)], rest[2]
            )
        ]
    if fetch is not None:
        halves, _, moments, group, lanes = prior_ref.shape
        known = prior_hbm.shape[0]
        copies = [
            pltpu.make_async_copy(
                prior_hbm.at[:, p, pl.ds(fetch * group, group), pl.ds(h * lanes, lanes)],
                prior_ref.at[h, p, pl.ds(0, known)],
                rest[2].at[2 * h + p],
            )
            for h in range(halves)
            for p in range(2)
        ]
    for copy in copies:
        copy.start()
    if fetch is not None:
        prior_ref[:, :, known:] = jnp.zeros((halves, 2, moments - known, group, lanes), F32)
    for v in range(vecs):
        columns = slice(v * width, (v + 1) * width)
        pieces = [cur_ref[cur_at + v], recv_a[:, columns], recv_b[:, columns]]
        used = blocks + 2 * rim
        if used < padded:
            pieces.append(jnp.zeros((padded - used, width), F32))
        high, low = split(jnp.concatenate(pieces, axis=0))
        source[v, 0:padded] = high
        source[v, padded : 2 * padded] = low
    for v in range(vecs):
        mixture = dot(mix_ref[...], source[v])
        high, low = split(mixture)
        for n in range(kind_count):
            columns = slice(n * width, (n + 1) * width)
            rows = slice(n * blocks, (n + 1) * blocks)
            mixed[v * blocks : (v + 1) * blocks, columns] = high[rows]
            mixed[(vecs + v) * blocks : (vecs + v + 1) * blocks, columns] = low[rows]
    count = vecs * blocks
    both = dot(mixed[...], high_ref[...])
    hopping = both[:count] + both[count:] + dot(mixed[:count], low_ref[...])
    diag_up = 2.0 * (site_ref[0] + site_ref[1])
    diag_down = 2.0 * (site_ref[0] - site_ref[1])
    cross = 2.0 * site_ref[2]
    partial = partial_in[...] if add_partial else None
    for v in range(vecs):
        here = cur_ref[cur_at + v]
        up = here[:, :spin]
        down = here[:, spin:]
        onsite = jnp.concatenate(
            [diag_up * up + cross * down, diag_down * down + cross * up], axis=1
        )
        following = hopping[v * blocks : (v + 1) * blocks] + onsite - prev_ref[prev_at + v]
        out_ref[v] = following
        term = probe_ref[own_at + v] * following
        partial = term if partial is None else partial + term
        if not last:
            columns = slice(v * width, (v + 1) * width)
            emit_sends(pick_ref[...], following, columns, send_a, send_b)
    partial_out[...] = partial
    if fold:
        quarter = blocks // 4
        for s, ref in enumerate(olders or [partial_out]):
            parts = [ref[i * quarter : (i + 1) * quarter] for i in range(4)]
            keep = [choose(index_ref, 1, *parts[2 * y : 2 * y + 2]) for y in range(2)]
            give = [choose(index_ref, 1, *parts[2 * y : 2 * y + 2][::-1]) for y in range(2)]
            if not older:
                pieces_out[0][...] = choose(index_ref, 2, *keep)
                pieces_out[1][...] = choose(index_ref, 2, *give)
                pieces_out[2][...] = choose(index_ref, 2, *keep[::-1])
                pieces_out[3][...] = choose(index_ref, 2, *give[::-1])
            else:
                for y in range(2):
                    keep_ref[s, y] = keep[y]
                    give_ref[s, y] = give[y]
    for copy in copies:
        copy.wait()


def fold_kernel(index_ref, keep_ref, got_ref, mine_ref, give_ref):
    for s in range(keep_ref.shape[0]):
        sums = [keep_ref[s, y] + got_ref[s, y] for y in range(2)]
        mine_ref[s] = choose(index_ref, 2, *sums)
        give_ref[s] = choose(index_ref, 2, *sums[::-1])


def energy_kernel(vector_total, chunks, count, even_ref, odd_ref, early_mine, early_got, *rest):
    priors, rest = rest[:count], rest[count:]
    lates, finals = rest[:4], rest[4 : 4 + chunks]
    new_ref, map_out, cur_out, fresh, held, sems = rest[4 + chunks :]
    halves, _, pairs, group, lanes = priors[0].shape
    vecs = finals[0].shape[0]
    copies = [
        pltpu.make_async_copy(
            finals[c], cur_out.at[pl.ds(c * vecs, vecs)], sems.at[count * halves + c]
        )
        for c in range(chunks)
    ]
    for copy in copies:
        copy.start()
    early = early_mine.shape[0]
    steps = new_ref.shape[0]
    scale = 1.0 / vector_total
    new_ref[0:early] = (early_mine[...] + early_got[...]) * scale
    new_ref[early] = ((lates[0][...] + lates[1][...]) + (lates[2][...] + lates[3][...])) * scale
    half = even_ref.shape[0]
    flip = 7 - lax.broadcasted_iota(jnp.int32, (8, lanes), 0)
    for i in range(count):
        for h in range(halves):
            slot = i * halves + h
            rows = slice(i * group, (i + 1) * group)
            columns = slice(h * lanes, (h + 1) * lanes)
            for p in range(2):
                fresh[slot, p, 0 : 8 - steps // 2] = jnp.zeros((8 - steps // 2, group, lanes), F32)
                for m in range(p, steps, 2):
                    fresh[slot, p, 8 - steps // 2 + m // 2] = new_ref[m, rows, columns]
            flat = held.at[slot].reshape(2 * half * group, lanes)
            for b in range(0, group, 2):
                sums = []
                for parity, table in ((0, even_ref), (1, odd_ref)):
                    pair = []
                    for j in range(2):
                        old = priors[i].at[h, parity].reshape(pairs * group, lanes)
                        value = old[pl.ds(b + j, pairs, stride=group)]
                        extra = fresh.at[slot, parity].reshape(8 * group, lanes)
                        added = extra[pl.ds(b + j, 8, stride=group)]
                        pair.append(
                            jnp.concatenate([value[: pairs - 8], value[pairs - 8 :] + added], axis=0)
                        )
                    high, low = split(jnp.concatenate(pair, axis=1))
                    sums.append(dot(table[...], jnp.concatenate([high, high, low, low], axis=0)))
                plus = sums[0] + sums[1]
                minus = sums[0] - sums[1]
                for j in range(2):
                    side = slice(j * lanes, (j + 1) * lanes)
                    flat[pl.ds(b + j, half, stride=group)] = plus[:, side]
                    for r in range(0, half, 8):
                        turned = jnp.take_along_axis(minus[r : r + 8, side], flip, axis=0)
                        top = 2 * half - 8 - r
                        flat[pl.ds(top * group + b + j, 8, stride=group)] = turned
            copy = pltpu.make_async_copy(
                held.at[slot],
                map_out.at[:, pl.ds(i * group, group), pl.ds(h * lanes, lanes)],
                sems.at[slot],
            )
            copy.start()
            copies.append(copy)
    for copy in copies:
        copy.wait()


def per_device(
    probe,
    cheb_prev,
    cheb_cur,
    prior_moments,
    site_terms,
    hop_kinds,
    tile_kind_ids,
    send_lists,
    tile_cols,
):
    group, lanes = 8, 128
    moment_count = prior_moments.shape[0] + STEPS
    vec_dev, blocks, width = cheb_cur.shape
    kind_count = hop_kinds.shape[0]
    groups = lax.axis_size("vec")
    domains = lax.axis_size("dom")
    rim = send_lists.shape[2]
    chunks = 2
    vecs = vec_dev // chunks
    quarter = blocks // groups
    padded = -(-(blocks + 2 * rim) // 256) * 256
    swap_a = [(i, i ^ 1) for i in range(domains)]
    swap_b = [(i, (i + 1) % domains if i % 2 else (i - 1) % domains) for i in range(domains)]
    vec_index = lax.axis_index("vec")
    index = jnp.stack([lax.axis_index("dom") % 2, vec_index % 2, vec_index // 2]).astype(jnp.int32)
    index = jnp.broadcast_to(index[:, None, None], (3, 8, 128))

    rows = jax.ShapeDtypeStruct((rim, vecs * width), F32)
    full_shape = jax.ShapeDtypeStruct((vec_dev, blocks, width), F32)
    chunk_shape = jax.ShapeDtypeStruct((vecs, blocks, width), F32)
    pick, cur_first, *sends = pl.pallas_call(
        functools.partial(first_kernel, rim),
        out_shape=[jax.ShapeDtypeStruct((2 * rim, 2 * blocks), BF16), chunk_shape, rows, rows],
        in_specs=[vmem(), hbm(), hbm()],
        out_specs=[vmem()] * 4,
        scratch_shapes=[
            pltpu.VMEM(send_lists.shape, jnp.int32),
            pltpu.SemaphoreType.DMA((vecs + 1,)),
        ],
        compiler_params=params(),
        cost_estimate=cost(1e8, 1e6),
        name="first_sends",
    )(index, stay(send_lists), stay(cheb_cur))

    def exchange(a, b):
        got_a = lax.ppermute(a, "dom", swap_a)
        got_b = lax.ppermute(b, "dom", swap_b)
        return got_a, got_b

    received = [exchange(*sends)]
    links = tile_cols.shape[1]
    mix, high, low, prev_held, probe_held, site_held, cur_second, *sends = pl.pallas_call(
        functools.partial(prep_kernel, rim),
        out_shape=[
            jax.ShapeDtypeStruct((kind_count * blocks, 2 * padded), BF16),
            jax.ShapeDtypeStruct((kind_count * width, width), BF16),
            jax.ShapeDtypeStruct((kind_count * width, width), BF16),
            full_shape,
            full_shape,
            jax.ShapeDtypeStruct(site_terms.shape, F32),
            chunk_shape,
            rows,
            rows,
        ],
        in_specs=[vmem(), hbm(), hbm(), vmem()] + [hbm()] * 5,
        out_specs=[vmem()] * 9,
        scratch_shapes=[
            pltpu.VMEM((links, blocks), jnp.int32),
            pltpu.VMEM((links, blocks), jnp.int32),
            pltpu.VMEM(hop_kinds.shape, F32),
            pltpu.SemaphoreType.DMA((kind_count + 5 + vecs,)),
        ],
        compiler_params=params(),
        cost_estimate=cost(1e7, 8e6),
        name="tables",
    )(
        index,
        stay(tile_cols.T),
        stay(tile_kind_ids.T),
        pick,
        *[stay(x) for x in (hop_kinds, cheb_cur, cheb_prev, probe, site_terms)],
    )
    received.append(exchange(*sends))

    partial_shape = jax.ShapeDtypeStruct((blocks, width), F32)
    current = [(cur_first, 0), (cur_second, 0)]
    previous = [(prev_held, c * vecs) for c in range(chunks)]

    def reduce(keep, give):
        got = lax.ppermute(give, "vec", [(i, i ^ 1) for i in range(groups)])
        piece = jax.ShapeDtypeStruct((keep.shape[0], quarter, width), F32)
        mine, give = pl.pallas_call(
            fold_kernel,
            out_shape=[piece, piece],
            in_specs=[vmem()] * 3,
            out_specs=[vmem()] * 2,
            compiler_params=params(),
            cost_estimate=cost(1e5, 1e6),
            name="fold",
        )(index, keep, got)
        return mine, lax.ppermute(give, "vec", [(i, i ^ 2) for i in range(groups)])

    partials = []
    buffers = []
    prior_held = []
    prior_pairs = prior_moments.reshape(prior_moments.shape[0] // 2, 2, quarter, width)
    for s in range(STEPS):
        last = s == STEPS - 1
        partial = None
        for c in range(chunks):
            args = [index, mix, high, low, pick, site_held]
            args += [current[c][0], previous[c][0], probe_held, *received[c]]
            specs = [vmem()] * len(args)
            fold = last
            older = len(partials) if fold and c == 0 else 0
            extra = ([] if partial is None else [partial]) + partials[:older]
            args += extra
            specs += [vmem()] * len(extra)
            place = s * chunks + c
            fetch = place if place < quarter // group else None
            if fetch is not None:
                args.append(stay(prior_pairs))
                specs.append(hbm())
            aliases = {len(args) + i: 2 + i for i in range(len(buffers))}
            args += buffers
            specs += [any_space()] * len(buffers)
            scratch = [
                pltpu.VMEM((vecs, 2 * padded, width), BF16),
                pltpu.VMEM((2 * vecs * blocks, kind_count * width), BF16),
            ]
            outs, out_specs = [chunk_shape, partial_shape], [vmem(), vmem()]
            if last:
                outs.append(full_shape)
                out_specs.append(any_space())
                scratch.append(pltpu.SemaphoreType.DMA)
            else:
                outs += [rows, rows]
            if fold and not older:
                outs += [jax.ShapeDtypeStruct((quarter, width), F32)] * 4
            elif fold:
                outs += [jax.ShapeDtypeStruct((older, groups // 2, quarter, width), F32)] * 2
            if fetch is not None:
                outs.append(
                    jax.ShapeDtypeStruct((width // lanes, 2, moment_count // 2, group, lanes), F32)
                )
                scratch.append(pltpu.SemaphoreType.DMA((2 * (width // lanes),)))
            out_specs += [vmem()] * (len(outs) - len(out_specs))
            cfg = (
                vecs,
                current[c][1],
                previous[c][1],
                c * vecs,
                last,
                partial is not None,
                older,
                fold,
                fetch,
                len(buffers),
            )
            result = list(
                pl.pallas_call(
                    functools.partial(step_kernel, cfg),
                    out_shape=outs,
                    in_specs=specs,
                    out_specs=out_specs,
                    scratch_shapes=scratch,
                    input_output_aliases=aliases,
                    compiler_params=pltpu.CompilerParams(vmem_limit_bytes=VMEM_LIMIT),
                    cost_estimate=cost(1.5e9, 5e6),
                )(*args)
            )
            previous[c], current[c] = current[c], (result.pop(0), 0)
            partial = result.pop(0)
            if last:
                buffers = [result.pop(0)]
            else:
                received[c] = exchange(result.pop(0), result.pop(0))
            if fetch is not None:
                prior_held.append(result.pop(0))
            if fold and not older:
                lates = [result[0]]
                for flip in (2, 3, 1):
                    pairs = [(i, i ^ flip) for i in range(groups)]
                    lates.append(lax.ppermute(result[flip], "vec", pairs))
            elif fold:
                early = reduce(*result)
        partials.append(partial)

    tables = [jnp.asarray(x) for x in jackson_split(moment_count, ENERGIES)]
    tiles = quarter // group * (width // lanes)
    args = [*tables, *early, *prior_held, *lates, *[current[c][0] for c in range(chunks)]]
    new_moments, energy_map, next_cur = pl.pallas_call(
        functools.partial(energy_kernel, vec_dev * groups, chunks, len(prior_held)),
        out_shape=[
            jax.ShapeDtypeStruct((STEPS, quarter, width), F32),
            jax.ShapeDtypeStruct((ENERGIES, quarter, width), F32),
            full_shape,
        ],
        in_specs=[vmem()] * len(args),
        out_specs=[vmem(), any_space(), any_space()],
        scratch_shapes=[
            pltpu.VMEM((tiles, 2, 8, group, lanes), F32),
            pltpu.VMEM((tiles, ENERGIES, group, lanes), F32),
            pltpu.SemaphoreType.DMA((tiles + chunks,)),
        ],
        compiler_params=params(),
        cost_estimate=cost(4e9, 2.2e7),
        name="energy",
    )(*args)
    return buffers[0], next_cur, new_moments, energy_map


def solution(mesh):
    return jax.shard_map(
        per_device,
        mesh=mesh,
        in_specs=(
            P("vec", "dom", None),
            P("vec", "dom", None),
            P("vec", "dom", None),
            P(None, ("dom", "vec"), None),
            P(None, "dom", None),
            P(),
            P("dom", None),
            P("dom", None, None),
            P("dom", None),
        ),
        out_specs=(
            P("vec", "dom", None),
            P("vec", "dom", None),
            P(None, ("dom", "vec"), None),
            P(None, ("dom", "vec"), None),
        ),
        check_vma=False,
    )
```
